128 devices in a mesh: cell: 16 (over x, z_hi, core), tm: 8 (over y, z_lo).
Axes of the slice: x: 4, y: 4, z: 4 (z_hi: 2, z_lo: 2; z = z_hi * 2 + z_lo), core: 2. Of those that a mesh axis runs over, the one named last changes fastest.
Arguments:
- window: float32 [16384, 16384], P('cell', 'tm'), may hold values from -0.09375 to 0.09375
- range_test: float32 [16384, 256], P('tm'), may hold values from -0.046875 to 0.046875
- co_test: float32 [256, 16384], P(None, 'cell'), may hold values from -0.046875 to 0.046875
- core_left: float32 [512, 16384], P(None, 'cell'), may hold values from -0.046875 to 0.046875
- core_right: float32 [512, 16384], P(None, 'tm'), may hold values from -0.046875 to 0.046875
Outputs:
- range_basis: float32 [16384, 256], P('cell')
- co_basis: float32 [256, 16384], P(None, 'tm')
- core: float32 [256, 256], replicated
The draws below stay inside these ranges and needn't reach their ends.
All inputs are finite; a program needn't handle non-finite values.
Results may differ from the reference program's by a relative error of at most 0.00023.
Values sent between devices are 32-bit elements; how exact they have to be, the bound alone decides.
A program may use at most 128 MiB of HBM per device.

```python
import math
import jax
import jax.numpy as jnp
from jax import lax

K = 256
L = 256
S_CORE = 512
M = 16384
N = 16384


def steps_of(own_key, extent, split, least, high):
    level = 1.0
    for position, blocks in split:
        draws = jax.random.uniform(jax.random.fold_in(jax.random.fold_in(own_key, 6), position), (blocks,), jnp.float32, least / len(split), high / len(split))
        level = level * jnp.repeat(jnp.exp(draws), extent[position] // blocks).reshape((-1,) + (1,) * (len(extent) - 1 - position))
    return level


def bell_draw(own_key, dims, scale, bound, cuts=(), held_as=jnp.bfloat16):
    values = jax.random.normal(own_key, dims, jnp.float32) * scale
    if len(cuts) > 0:
        values = steps_of(own_key, dims, cuts, -0.22, 0.18) * values
    return jnp.clip(values, min=-bound, max=bound).astype(held_as)


def setup_inputs(seed: int = 0) -> dict:
    streams_of = jax.random.split(jax.random.key(seed), 6)
    window = bell_draw(streams_of[0], (M, N), (M * N // ((S_CORE - K) * (S_CORE - L))) ** -0.5, 0.09375, ((0, 16), (1, 8)), jnp.float32)
    range_test = bell_draw(streams_of[1], (N, K), N ** -0.5, 0.046875, ((0, 8),), jnp.float32)
    co_test = bell_draw(streams_of[2], (L, M), M ** -0.5, 0.046875, ((1, 16),), jnp.float32)
    core_left = bell_draw(streams_of[3], (S_CORE, M), M ** -0.5, 0.046875, ((1, 16),), jnp.float32)
    core_right = bell_draw(streams_of[4], (S_CORE, N), N ** -0.5, 0.046875, ((1, 8),), jnp.float32)
    return dict(window=window, range_test=range_test, co_test=co_test, core_left=core_left, core_right=core_right)


def reference(window, range_test, co_test, core_left, core_right):
    highest = lax.Precision.HIGHEST
    sketch_y = jnp.dot(window.astype(jnp.float32), range_test.astype(jnp.float32), precision=highest, preferred_element_type=jnp.float32)
    sketch_w = jnp.dot(co_test.astype(jnp.float32), window.astype(jnp.float32), precision=highest, preferred_element_type=jnp.float32)
    left_window = jnp.dot(core_left.astype(jnp.float32), window.astype(jnp.float32), precision=highest, preferred_element_type=jnp.float32)
    sketch_z = lax.dot_general(left_window, core_right, (((1,), (1,)), ((), ())), precision=highest)
    gram_y = lax.dot_general(sketch_y, sketch_y, (((0,), (0,)), ((), ())), precision=highest) / M
    gram_w = lax.dot_general(sketch_w, sketch_w, (((1,), (1,)), ((), ())), precision=highest) / N
    lower_y = jnp.linalg.cholesky(gram_y)
    lower_w = jnp.linalg.cholesky(gram_w)
    range_basis = jax.scipy.linalg.solve_triangular(lower_y, sketch_y.T, lower=True).T
    co_basis = jax.scipy.linalg.solve_triangular(lower_w, sketch_w, lower=True)
    left_image = jnp.dot(core_left, range_basis, precision=highest)
    right_image = lax.dot_general(core_right, co_basis, (((1,), (1,)), ((), ())), precision=highest)
    gram_left = jnp.dot(left_image.T, left_image, precision=highest)
    gram_right = jnp.dot(right_image.T, right_image, precision=highest)
    projected = jnp.dot(left_image.T, sketch_z, precision=highest)
    left_solved = jax.scipy.linalg.cho_solve((jnp.linalg.cholesky(gram_left), True), projected)
    middle = jnp.dot(left_solved, right_image, precision=highest)
    core = jax.scipy.linalg.cho_solve((jnp.linalg.cholesky(gram_right), True), middle.T).T
    core = core * math.sqrt(M * N)
    return (range_basis, co_basis, core)
```

```python
import functools
import math

import jax
import jax.numpy as jnp
from jax import lax
from jax.experimental import pallas as pl
from jax.experimental.pallas import tpu as pltpu
from jax.sharding import PartitionSpec as P

MESH = pl.DeviceIdType.MESH
F32 = jnp.float32
BF16 = jnp.bfloat16
NN = (((1,), (0,)), ((), ()))
NT = (((1,), (1,)), ((), ()))
TN = (((0,), (0,)), ((), ()))


def split(value):
    high = value.astype(BF16)
    low = (value - high.astype(F32)).astype(BF16)
    return high, low


def mm(left, right, dims):
    return lax.dot_general(left, right, dims, preferred_element_type=F32)


def mm3(left, right, dims):
    return mm(left[0], right[0], dims) + (mm(left[0], right[1], dims) + mm(left[1], right[0], dims))


def mm3f(left, right, dims):
    return mm3(split(left), split(right), dims)


def mmh(left, right, dims):
    return lax.dot_general(left, right, dims, precision=lax.Precision.HIGHEST, preferred_element_type=F32)


class Reduce:
    def __init__(self, net, source, out, core_in, total, relay_a, relay_b, in_l, in_r, y_in, z_in, rows):
        self.net, self.source, self.out = net, source, out
        self.core_in, self.total = core_in, total
        self.ra, self.rb, self.in_l, self.in_r = relay_a, relay_b, in_l, in_r
        self.y_in, self.z_in, self.r = y_in, z_in, rows

    def core_send(self):
        n, r = self.net, self.r
        self.c = n.copy(self.source.at[n.rows((1 - n.c) * 16 * r, 16 * r)], self.core_in, n.partner)

    def core_done(self):
        n, r = self.net, self.r
        self.c.wait_recv()
        self.total[...] = self.source[n.rows(n.c * 16 * r, 16 * r), :] + self.core_in[...]
        self.ring = RingScatter(n, "x", self.total, 4 * r, self.ra, self.rb, self.in_l, self.in_r)
        self.ring.first()
        self.ring.second()
        self.ring.third()

    def x_mid(self):
        self.ring.mid()

    def x_done(self):
        n, r = self.net, self.r
        self.ring.finish()
        base = n.x * 4 * r
        own = n.rows(base, 4 * r)
        self.total[own, :] = self.total[own, :] + (self.in_l[...] + self.in_r[...])
        self.y = []
        for k in (1, 2, 3):
            q = lax.rem(n.y + k, 4)
            self.y.append(n.copy(self.total.at[n.rows(base + q * r, r)], self.y_in.at[k - 1], n.at(y=q)))

    def y_done(self):
        n, r = self.net, self.r
        for c in self.y:
            c.wait_recv()
        own = n.rows(n.x * 4 * r + n.y * r, r)
        self.z_in[n.z] = (self.total[own, :] + self.y_in[0]) + (self.y_in[1] + self.y_in[2])
        self.zc = []
        for k in (1, 2, 3):
            self.zc.append(n.copy(self.z_in.at[n.z], self.z_in.at[n.z], n.at(z=lax.rem(n.z + k, 4))))

    def z_done(self):
        n, r = self.net, self.r
        for c in self.zc:
            c.wait_recv()
        offset = n.c * 16 * r + n.x * 4 * r + n.y * r
        own = n.rows(offset, r)
        self.out[own, :] = (self.z_in[0] + self.z_in[1]) + (self.z_in[2] + self.z_in[3])
        self.yc = []
        for k in (1, 2, 3):
            self.yc.append(n.copy(self.out.at[own], self.out.at[own], n.at(y=lax.rem(n.y + k, 4))))

    def y_gathered(self):
        n, r = self.net, self.r
        for c in self.yc:
            c.wait_recv()
        self.gather = RingGather(n, "x", self.out, n.c * 16 * r, 4 * r)
        self.gather.first()

    def x_gather_mid(self):
        self.gather.mid()

    def x_gathered(self):
        n, r = self.net, self.r
        self.gather.finish()
        own = n.rows(n.c * 16 * r, 16 * r)
        self.c2 = n.copy(self.out.at[own], self.out.at[own], n.partner)

    def core_gathered(self):
        self.c2.wait_recv()


class RingScatter:
    def __init__(self, net, axis, parts, size, relay_a, relay_b, in_l, in_r):
        self.n, self.parts, self.size, self.half = net, parts, size, size // 2
        me = getattr(net, axis)
        self.far, self.right, self.left = lax.rem(me + 2, 4), lax.rem(me + 1, 4), lax.rem(me + 3, 4)
        self.to_right, self.to_left = net.at(**{axis: self.right}), net.at(**{axis: self.left})
        self.ra, self.rb, self.in_l, self.in_r = relay_a, relay_b, in_l, in_r

    def piece(self, q, side):
        return self.n.rows(q * self.size + side * self.half, self.half)

    def first(self):
        self.c0 = self.n.copy(self.parts.at[self.piece(self.far, 0)], self.ra, self.to_right)
        self.c1 = self.n.copy(self.parts.at[self.piece(self.far, 1)], self.rb, self.to_left)

    def second(self):
        h = self.half
        self.c2 = self.n.copy(self.parts.at[self.piece(self.right, 1)], self.in_l.at[pl.ds(h, h)], self.to_right)

    def third(self):
        h = self.half
        self.c3 = self.n.copy(self.parts.at[self.piece(self.left, 0)], self.in_r.at[pl.ds(0, h)], self.to_left)

    def mid(self):
        h = self.half
        self.c0.wait_recv()
        at = self.piece(self.right, 0)
        self.parts[at, :] = self.parts[at, :] + self.ra[...]
        self.c4 = self.n.copy(self.parts.at[at], self.in_l.at[pl.ds(0, h)], self.to_right)
        self.c1.wait_recv()
        at = self.piece(self.left, 1)
        self.parts[at, :] = self.parts[at, :] + self.rb[...]
        self.c5 = self.n.copy(self.parts.at[at], self.in_r.at[pl.ds(h, h)], self.to_left)

    def finish(self):
        for c in (self.c2, self.c3, self.c4, self.c5):
            c.wait_recv()


class RingGather:
    def __init__(self, net, axis, out, base, size):
        self.n, self.out, self.base, self.size, self.half = net, out, base, size, size // 2
        self.me = getattr(net, axis)
        self.right, self.left = lax.rem(self.me + 1, 4), lax.rem(self.me + 3, 4)
        self.to_right, self.to_left = net.at(**{axis: self.right}), net.at(**{axis: self.left})

    def first(self):
        own = self.n.rows(self.base + self.me * self.size, self.size)
        self.g0 = self.n.copy(self.out.at[own], self.out.at[own], self.to_right)
        self.g1 = self.n.copy(self.out.at[own], self.out.at[own], self.to_left)

    def mid(self):
        self.g0.wait_recv()
        at = self.n.rows(self.base + self.left * self.size, self.half)
        self.g2 = self.n.copy(self.out.at[at], self.out.at[at], self.to_right)
        self.g1.wait_recv()
        at = self.n.rows(self.base + self.right * self.size + self.half, self.half)
        self.g3 = self.n.copy(self.out.at[at], self.out.at[at], self.to_left)

    def finish(self):
        self.g2.wait_recv()
        self.g3.wait_recv()


class Net:
    def __init__(self, send_sem, recv_sem):
        cell, tm = lax.axis_index("cell"), lax.axis_index("tm")
        self.x, self.zh, self.c = cell // 4, lax.rem(cell // 2, 2), lax.rem(cell, 2)
        self.y, self.zl = tm // 2, lax.rem(tm, 2)
        self.z = self.zh * 2 + self.zl
        self.partner = self.at(c=1 - self.c)
        self.send_sem, self.recv_sem = send_sem, recv_sem
        self.copies = []

    def at(self, x=None, y=None, z=None, c=None):
        x = self.x if x is None else x
        y = self.y if y is None else y
        c = self.c if c is None else c
        zh, zl = (self.zh, self.zl) if z is None else (z // 2, lax.rem(z, 2))
        return ((x * 2 + zh) * 2 + c, y * 2 + zl)

    def rows(self, start, size):
        return pl.ds(pl.multiple_of(start, 8), size)

    def copy(self, src, dst, device):
        k = len(self.copies)
        c = pltpu.make_async_remote_copy(
            src_ref=src, dst_ref=dst, send_sem=self.send_sem.at[k], recv_sem=self.recv_sem.at[k],
            device_id=device, device_id_type=MESH,
        )
        c.start()
        self.copies.append(c)
        return c


COPIES = 80


def order(k):
    return lax.rem(2 + 3 * k + (k // 2) * (3 + 2 * lax.rem(k, 2)), 4)


def exchange_kernel(
    window, range_test, co_test, core_left, core_right,
    y_out, w_out, cycw_out, late_out,
    w_stage, w_hi, w_lo, rt_f, ct_f, cl_f, cr_f, rt_hi, rt_lo, ct_hi, ct_lo, cl_hi, cl_lo, cr_hi, cr_lo,
    co, co_hi, co_lo, co_core, co_ra, co_rb, co_l, co_r, co_z,
    rg, rg_hi, rg_lo, rg_ra, rg_rb, rg_l, rg_r, rg_z,
    v_hi, v_lo, z_hi, z_lo,
    ar1, a1_core, a1_tot, a1_ra, a1_rb, a1_l, a1_r, a1_y, a1_z,
    ar2, a2_core, a2_tot, a2_ra, a2_rb, a2_l, a2_r, a2_y, a2_z,
    in_sem, send_sem, recv_sem,
):
    n = Net(send_sem, recv_sem)
    barrier = pltpu.get_barrier_semaphore()
    peers = [n.partner]
    for k in (1, 2, 3):
        peers += [n.at(x=lax.rem(n.x + k, 4)), n.at(y=lax.rem(n.y + k, 4)), n.at(z=lax.rem(n.z + k, 4))]
    for peer in peers:
        pl.semaphore_signal(barrier, inc=1, device_id=peer, device_id_type=MESH)

    def column_block(s):
        return ((1 - s // 4) * (1 - n.c) + (s // 4) * n.c) * 4 + lax.rem(n.x + order(lax.rem(s, 4)), 4)

    def w_copy(s):
        return pltpu.make_async_copy(
            window.at[:, pl.ds(pl.multiple_of(column_block(s) * 256, 256), 256)], w_stage.at[s], in_sem.at[s])

    loads = [pltpu.make_async_copy(a, b, in_sem.at[8 + i]) for i, (a, b) in enumerate(
        ((co_test, ct_f), (range_test, rt_f), (core_left, cl_f), (core_right, cr_f)))]
    loads[0].start()
    for s in range(8):
        w_copy(s).start()
    for c in loads[1:]:
        c.start()

    loads[0].wait()
    ct_hi[...], ct_lo[...] = split(ct_f[...])

    def co_block(s):
        w_copy(s).wait()
        block = column_block(s)
        cols = pl.ds(pl.multiple_of(block * 256, 256), 256)
        for part in range(2):
            rows = pl.ds(part * 512, 512)
            high, low = split(w_stage[s, rows, :])
            w_hi[rows, cols] = high
            w_lo[rows, cols] = low
        value = mm3((ct_hi[...], ct_lo[...]), (w_hi[:, cols], w_lo[:, cols]), NN)
        co_hi[block], co_lo[block] = split(value)
        at = n.rows(block * 512, 256)
        co[at, :] = value[:, :128]
        at = n.rows(block * 512 + 256, 256)
        co[at, :] = value[:, 128:]

    co_copies = []
    pl.loop(0, 4)(co_block)
    pl.semaphore_wait(barrier, 10)
    co_core_copy = n.copy(co.at[n.rows((1 - n.c) * 2048, 2048)], co_core, n.partner)
    pl.loop(4, 8)(co_block)

    loads[1].wait()
    rt_hi[...], rt_lo[...] = split(rt_f[...])
    co_core_copy.wait_recv()
    co_core[...] = co_core[...] + co[n.rows(n.c * 2048, 2048), :]
    co_ring = RingScatter(n, "x", co_core, 512, co_ra, co_rb, co_l, co_r)
    co_ring.first()
    co_ring.second()
    co_ring.third()

    rg_ring = RingScatter(n, "y", rg, 256, rg_ra, rg_rb, rg_l, rg_r)

    def range_block(k):
        rows = n.rows(lax.rem(n.y + order(k), 4) * 256, 256)
        value = mm3((w_hi[rows, :], w_lo[rows, :]), (rt_hi[...], rt_lo[...]), NN)
        rg[rows, :] = value
        rg_hi[rows, :], rg_lo[rows, :] = split(value)

    pl.loop(0, 3)(range_block)
    rg_ring.first()
    rg_ring.second()
    rg_ring.third()
    pl.loop(3, 4)(range_block)
    co_ring.mid()

    loads[2].wait()
    cl_hi[...], cl_lo[...] = split(cl_f[...])
    ar1[pl.ds(0, 512), :] = mm3((cl_hi[...], cl_lo[...]), (rg_hi[...], rg_lo[...]), NN)
    loads[3].wait()
    cr_hi[...], cr_lo[...] = split(cr_f[...])
    rg_ring.mid()
    ar1[pl.ds(512, 512), :] = jnp.zeros((512, 256), F32)

    def cw_block(k):
        cols = pl.ds(pl.multiple_of(k * 256, 256), 256)
        ar1[pl.ds(512, 512), :] += mm3((cr_hi[:, cols], cr_lo[:, cols]), (co_hi[k], co_lo[k]), NT)

    pl.loop(0, 8)(cw_block)
    first = Reduce(n, ar1, cycw_out, a1_core, a1_tot, a1_ra, a1_rb, a1_l, a1_r, a1_y, a1_z, 32)
    first.core_send()

    def v_block(k):
        rows = n.rows(k * 256, 256)
        value = mm3((w_hi[rows, :], w_lo[rows, :]), (cr_hi[...], cr_lo[...]), NT)
        v_hi[rows, :], v_lo[rows, :] = split(value)

    pl.loop(0, 1)(v_block)
    co_ring.finish()
    own = n.rows(n.x * 512, 512)
    co_core[own, :] = co_core[own, :] + (co_l[...] + co_r[...])
    co_z_copy = n.copy(co_core.at[n.rows(n.x * 512 + (1 - n.zh) * 256, 256)], co_z, n.at(z=lax.rem(n.z + 2, 4)))
    first.core_done()
    pl.loop(1, 2)(v_block)
    rg_ring.finish()
    own = n.rows(n.y * 256, 256)
    rg[own, :] = rg[own, :] + (rg_l[...] + rg_r[...])
    rg_z_copy = n.copy(rg.at[n.rows(n.y * 256 + (1 - n.zl) * 128, 128)], rg_z, n.at(z=n.zh * 2 + 1 - n.zl))
    co_z_copy.wait_recv()
    w_block = n.c * 8 + n.x * 2 + n.zh
    w_own = n.rows(w_block * 256, 256)
    w_out[w_own, :] = co_core[n.rows(n.x * 512 + n.zh * 256, 256), :] + co_z[...]
    w_z_copy = n.copy(w_out.at[w_own], w_out.at[w_own], n.at(z=lax.rem(n.z + 2, 4)))
    first.x_mid()
    pl.loop(2, 3)(v_block)
    rg_z_copy.wait_recv()
    y_own = n.rows(n.y * 256 + n.zl * 128, 128)
    y_out[y_own, :] = rg[y_own, :] + rg_z[...]
    y_z_copy = n.copy(y_out.at[y_own], y_out.at[y_own], n.at(z=n.zh * 2 + 1 - n.zl))
    first.x_done()

    part = split(y_out[y_own, :])
    ar2[pl.ds(0, 256), :] = mm3(part, part, TN) * (1.0 / 16384)
    part = split(w_out[w_own, :])
    ar2[pl.ds(256, 256), :] = mm3(part, part, NT) * (1.0 / 16384)
    w_z_copy.wait_recv()
    w_gather = RingGather(n, "x", w_out, n.c * 2048, 512)
    w_gather.first()
    pl.loop(3, 4)(v_block)
    first.y_done()
    y_z_copy.wait_recv()
    y_gather = RingGather(n, "y", y_out, 0, 256)
    y_gather.first()

    def z_block(k):
        rows = n.rows(k * 256, 256)
        value = mm3((cl_hi[rows, :], cl_lo[rows, :]), (v_hi[...], v_lo[...]), NN)
        z_hi[rows, :], z_lo[rows, :] = split(value)

    pl.loop(0, 2)(z_block)
    first.z_done()
    w_gather.mid()
    first.y_gathered()
    y_gather.mid()
    first.x_gather_mid()
    first.x_gathered()
    w_gather.finish()
    w_half = n.rows(n.c * 2048, 2048)
    w_core_copy = n.copy(w_out.at[w_half], w_out.at[w_half], n.partner)
    first.core_gathered()

    middle = mm3((z_hi[...], z_lo[...]), split(cycw_out[pl.ds(512, 512), :]), NN)
    ar2[pl.ds(512, 256), :] = mm3f(cycw_out[pl.ds(0, 512), :], middle, TN)
    second = Reduce(n, ar2, late_out, a2_core, a2_tot, a2_ra, a2_rb, a2_l, a2_r, a2_y, a2_z, 24)
    second.core_send()
    second.core_done()
    second.x_mid()
    second.x_done()
    second.y_done()
    second.z_done()
    second.y_gathered()
    second.x_gather_mid()
    second.x_gathered()
    y_gather.finish()
    w_core_copy.wait_recv()
    second.core_gathered()
    for c in n.copies:
        c.wait_send()


def exchange(window, range_test, co_test, core_left, core_right):
    def f(*shape):
        return pltpu.VMEM(shape, F32)

    def b(*shape):
        return pltpu.VMEM(shape, BF16)

    def reduce_bufs(r):
        return [f(16 * r, 256), f(16 * r, 256), f(2 * r, 256), f(2 * r, 256), f(4 * r, 256), f(4 * r, 256),
                f(3, r, 256), f(4, r, 256)]

    scratch = [
        f(8, 1024, 256), b(1024, 2048), b(1024, 2048), f(2048, 256), f(256, 1024), f(512, 1024), f(512, 2048),
        b(2048, 256), b(2048, 256), b(256, 1024), b(256, 1024), b(512, 1024), b(512, 1024), b(512, 2048), b(512, 2048),
        f(4096, 128), b(8, 256, 256), b(8, 256, 256), f(2048, 128), f(256, 128), f(256, 128), f(512, 128), f(512, 128), f(256, 128),
        f(1024, 256), b(1024, 256), b(1024, 256), f(128, 256), f(128, 256), f(256, 256), f(256, 256), f(128, 256),
        b(1024, 512), b(1024, 512), b(512, 512), b(512, 512),
        f(1024, 256), *reduce_bufs(32),
        f(768, 256), *reduce_bufs(24),
        pltpu.SemaphoreType.DMA((12,)), pltpu.SemaphoreType.DMA((COPIES,)), pltpu.SemaphoreType.DMA((COPIES,)),
    ]
    return pl.pallas_call(
        exchange_kernel,
        out_shape=[jax.ShapeDtypeStruct(s, F32) for s in ((1024, 256), (4096, 128), (1024, 256), (768, 256))],
        in_specs=[pl.BlockSpec(memory_space=pl.ANY)] * 5,
        out_specs=[pl.BlockSpec(memory_space=pltpu.VMEM)] * 4,
        scratch_shapes=scratch,
        compiler_params=pltpu.CompilerParams(collective_id=0, has_side_effects=True, vmem_limit_bytes=67043328),
        name="exchange",
    )(window, range_test, co_test, core_left, core_right)


QUAD = 4


def factor_panel(tiles):
    lane = lax.broadcasted_iota(jnp.int32, (8, 128), 1)
    sub = lax.broadcasted_iota(jnp.int32, (8, 128), 0)
    group = (lane // 32) * 32
    p = list(tiles)
    e = [jnp.where(sub + 8 * t == lane - group, 1.0, 0.0).astype(F32) for t in range(4)]
    pivots = [None] * 32

    def row(x, s):
        return jnp.broadcast_to(x[s:s + 1, :], (8, 128))

    for j in range(0, 32, QUAD):
        t0 = j // 8
        cols = [[jnp.take_along_axis(p[t], group + (j + k), axis=1) for t in range(t0, 4)] for k in range(QUAD)]
        rows = [row(p[t0], j % 8 + k) for k in range(QUAD)]
        rows_e = [row(e[t0], j % 8 + k) for k in range(QUAD)]
        s = [[row(cols[k][0], j % 8 + l) for l in range(QUAD)] for k in range(QUAD)]
        coefs = []
        for k in range(QUAD):
            d = s[k][k]
            pivots[j + k] = d
            inv = 1.0 / d
            for l in range(k + 1, QUAD):
                f = s[k][l] * inv
                for m in range(l, QUAD):
                    s[l][m] = s[l][m] - s[k][m] * f
                cols[l] = [a - b * f for a, b in zip(cols[l], cols[k])]
                rows[l] = rows[l] - rows[k] * f
                rows_e[l] = rows_e[l] - rows_e[k] * f
            coefs.append(inv)
        for i, t in enumerate(range(t0, 4)):
            for k in range(QUAD):
                coef = cols[k][i] * coefs[k]
                if t == t0:
                    coef = jnp.where(sub > j % 8 + k, coef, 0.0)
                p[t] = p[t] - coef * rows[k]
                e[t] = e[t] - coef * rows_e[k]
    out = []
    for t in range(4):
        d = pivots[8 * t]
        for s in range(1, 8):
            d = jnp.where(sub == s, pivots[8 * t + s], d)
        out.append(e[t] * (1.0 / jnp.sqrt(d)))
    return out


def final_kernel(y_ref, w_ref, cycw, late, rb_ref, cb_ref, core_ref, mat):
    lane = lax.broadcasted_iota(jnp.int32, (32, 128), 1)
    eye = (lax.broadcasted_iota(jnp.int32, (256, 256), 0) == lax.broadcasted_iota(jnp.int32, (256, 256), 1)).astype(F32)
    mat[0, :, 0:256] = late[pl.ds(0, 256), :]
    mat[1, :, 0:256] = late[pl.ds(256, 256), :]
    for m in (2, 3):
        part = split(cycw[pl.ds((m - 2) * 512, 512), :])
        mat[m, :, 0:256] = mm3(part, part, TN)
    for m in range(4):
        mat[m, :, 256:512] = eye
    for p in range(8):
        r0 = 32 * p
        c0 = r0 // 128 * 128
        packed = None
        for m in range(4):
            block = mat[m, r0:r0 + 32, c0:c0 + 128]
            shift = (m * 32 - r0 % 128) % 128
            if shift:
                block = pltpu.roll(block, shift, axis=1)
            packed = block if packed is None else jnp.where(lane // 32 == m, block, packed)
        inverse = jnp.concatenate(factor_panel([packed[8 * t:8 * t + 8, :] for t in range(4)]), axis=0)
        left = jnp.concatenate([jnp.where(lane // 32 == m, inverse, 0.0) for m in range(4)], axis=0)
        right = jnp.concatenate([mat[m, r0:r0 + 32, :] for m in range(4)], axis=0)
        upper = mmh(left, right, NN)
        for m in range(4):
            mat[m, r0:r0 + 32, :] = upper[32 * m:32 * m + 32, :]
        if p == 7:
            break
        b0 = (r0 + 32) // 128 * 128
        e1 = 256 + (r0 + 32 + 127) // 128 * 128
        for m in range(4):
            u = upper[32 * m:32 * m + 32, :]
            ut = u[:, b0:256].T[r0 + 32 - b0:, :]
            mat[m, r0 + 32:, b0:e1] = mat[m, r0 + 32:, b0:e1] - mmh(ut, u[:, b0:e1], NN)
    keep = lax.broadcasted_iota(jnp.int32, (256, 256), 0) <= lax.broadcasted_iota(jnp.int32, (256, 256), 1)
    y_inv = split(mat[0, :, 256:512])
    w_inv = split(mat[1, :, 256:512])
    for k in range(4):
        rb_ref[256 * k:256 * k + 256, :] = mm3(split(y_ref[256 * k:256 * k + 256, :]), y_inv, NT)
    for k in range(16):
        cb_ref[:, 128 * k:128 * k + 128] = mm3(w_inv, split(w_ref[256 * k:256 * k + 256, :]), NN)
    up_y = jnp.where(keep, mat[0, :, 0:256], 0.0)
    up_w = jnp.where(keep, mat[1, :, 0:256], 0.0)
    l_inv = mat[2, :, 256:512]
    r_inv = mat[3, :, 256:512]
    left = mmh(up_y, mmh(l_inv, l_inv, TN), NN)
    right = mmh(mmh(r_inv, r_inv, TN), up_w, NT)
    core_ref[...] = mmh(mmh(left, late[pl.ds(512, 256), :], NN), right, NN) * 16384.0


def final(y, w, cycw, late):
    return pl.pallas_call(
        final_kernel,
        out_shape=[jax.ShapeDtypeStruct(s, F32) for s in ((1024, 256), (256, 2048), (256, 256))],
        in_specs=[pl.BlockSpec(memory_space=pltpu.VMEM)] * 4,
        out_specs=[pl.BlockSpec(memory_space=pltpu.VMEM)] * 3,
        scratch_shapes=[pltpu.VMEM((4, 256, 512), F32)],
        compiler_params=pltpu.CompilerParams(vmem_limit_bytes=60000000),
        name="final",
    )(y, w, cycw, late)


def per_device(window, range_test, co_test, core_left, core_right):
    return tuple(final(*exchange(window, range_test, co_test, core_left, core_right)))


def solution(mesh):
    return jax.shard_map(
        per_device,
        mesh=mesh,
        in_specs=(P("cell", "tm"), P("tm", None), P(None, "cell"), P(None, "cell"), P(None, "tm")),
        out_specs=(P("cell", None), P(None, "tm"), P()),
        check_vma=False,
    )
```

```python
import functools
import math

import jax
import jax.numpy as jnp
from jax import lax
from jax.experimental import pallas as pl
from jax.experimental.pallas import tpu as pltpu
from jax.sharding import PartitionSpec as P

MESH = pl.DeviceIdType.MESH
F32 = jnp.float32
BF16 = jnp.bfloat16
NN = (((1,), (0,)), ((), ()))
NT = (((1,), (1,)), ((), ()))
TN = (((0,), (0,)), ((), ()))


def split(value):
    high = value.astype(BF16)
    low = (value - high.astype(F32)).astype(BF16)
    return high, low


def mm(left, right, dims):
    return lax.dot_general(left, right, dims, preferred_element_type=F32)


def mm3(left, right, dims):
    return mm(left[0], right[0], dims) + (mm(left[0], right[1], dims) + mm(left[1], right[0], dims))


def mm3f(left, right, dims):
    return mm3(split(left), split(right), dims)


def mmh(left, right, dims):
    return lax.dot_general(left, right, dims, precision=lax.Precision.HIGHEST, preferred_element_type=F32)


class Net:
    def __init__(self, send_sem, recv_sem):
        cell, tm = lax.axis_index("cell"), lax.axis_index("tm")
        self.x, self.zh, self.c = cell // 4, lax.rem(cell // 2, 2), lax.rem(cell, 2)
        self.y, self.zl = tm // 2, lax.rem(tm, 2)
        self.z = self.zh * 2 + self.zl
        self.flip = self.zh * 2 + 1 - self.zl
        self.partner = self.at(c=1 - self.c)
        self.send_sem, self.recv_sem = send_sem, recv_sem
        self.copies = []

    def at(self, x=None, y=None, z=None, c=None):
        x = self.x if x is None else x
        y = self.y if y is None else y
        c = self.c if c is None else c
        zh, zl = (self.zh, self.zl) if z is None else (z // 2, lax.rem(z, 2))
        return ((x * 2 + zh) * 2 + c, y * 2 + zl)

    def step(self, axis, k):
        return getattr(self, axis) if k == 0 else lax.rem(getattr(self, axis) + k, 4)

    def rows(self, start, size):
        return pl.ds(pl.multiple_of(start, 8), size)

    def copy(self, src, dst, device):
        k = len(self.copies)
        c = pltpu.make_async_remote_copy(
            src_ref=src, dst_ref=dst, send_sem=self.send_sem.at[k], recv_sem=self.recv_sem.at[k],
            device_id=device, device_id_type=MESH,
        )
        c.start()
        self.copies.append(c)
        return c


PAIRS = [(i, j) for i in (2, 1, 3, 0) for j in (2, 1, 3, 0) if i or j]


class Reduce:
    def __init__(self, net, plane, third, rows, source, out, core_in, plane_in, third_in):
        self.net, self.plane, self.third, self.r = net, plane, third, rows
        self.source, self.out = source, out
        self.core_in, self.plane_in, self.third_in = core_in, plane_in, third_in

    def place(self, i, j):
        a, b = self.plane
        return self.net.c * 16 * self.r + (self.net.step(a, i) * 4 + self.net.step(b, j)) * self.r

    def peer(self, i, j):
        a, b = self.plane
        return self.net.at(**{a: self.net.step(a, i), b: self.net.step(b, j)})

    def core_send(self):
        n, half = self.net, 16 * self.r
        self.c = n.copy(self.source.at[n.rows((1 - n.c) * half, half)], self.core_in, n.partner)

    def core_done(self):
        n, r = self.net, self.r
        self.c.wait_recv()
        own = n.rows(n.c * 16 * r, 16 * r)
        self.source[own, :] = self.source[own, :] + self.core_in[...]
        self.p = [n.copy(self.source.at[n.rows(self.place(i, j), r)], self.plane_in.at[k], self.peer(i, j))
                  for k, (i, j) in enumerate(PAIRS)]

    def plane_done(self):
        n, r = self.net, self.r
        total = self.source[n.rows(self.place(0, 0), r), :]
        for k, c in enumerate(self.p):
            c.wait_recv()
            total = total + self.plane_in[k]
        me = getattr(n, self.third)
        self.third_in[me] = total
        self.t = [n.copy(self.third_in.at[me], self.third_in.at[me], n.at(**{self.third: n.step(self.third, k)}))
                  for k in (2, 1, 3)]

    def third_done(self):
        n, r = self.net, self.r
        for c in self.t:
            c.wait_recv()
        own = n.rows(self.place(0, 0), r)
        self.out[own, :] = (self.third_in[0] + self.third_in[1]) + (self.third_in[2] + self.third_in[3])
        self.g = [n.copy(self.out.at[own], self.out.at[own], self.peer(i, j)) for i, j in PAIRS]

    def gathered(self):
        n, half = self.net, 16 * self.r
        for c in self.g:
            c.wait_recv()
        own = n.rows(n.c * half, half)
        self.c2 = n.copy(self.out.at[own], self.out.at[own], n.partner)

    def core_gathered(self):
        self.c2.wait_recv()


COPIES = 140
ORDER = (2, 1, 3, 0)
PLANES = ((("x", "y"), "z"), (("x", "y"), "z"), (("x", "y"), "z"))


def meet(n):
    barrier = pltpu.get_barrier_semaphore()
    peers = [n.partner]
    for axis in "xyz":
        peers += [n.at(**{axis: n.step(axis, k)}) for k in (1, 2, 3)]
    planes = set(p for p, _ in PLANES)
    for a, b in sorted(planes):
        peers += [n.at(**{a: n.step(a, i), b: n.step(b, j)}) for i in (1, 2, 3) for j in (1, 2, 3)]
    if ("y", "z") not in planes:
        peers += [n.at(y=n.step("y", k), z=n.flip) for k in (1, 2, 3)]
    for peer in peers:
        pl.semaphore_signal(barrier, inc=1, device_id=peer, device_id_type=MESH)
    return barrier, len(peers)


def exchange_kernel(
    window, range_test, co_test, core_left, core_right,
    y_out, w_out, gram_out, cyw_out, z_out,
    w_stage, w_hi, w_lo, rt_f, ct_f, cl_f, cr_f, rt_hi, rt_lo, ct2, cl_hi, cl_lo, cr_hi, cr_lo,
    co, co_core, co_in, co_z, rg, rg_hi, rg_lo, rg_in, v_hi, v_lo,
    gram, g_core, g_plane, g_third, cyw, c_core, c_plane, c_third, zed, z_core, z_plane, z_third,
    in_sem, send_sem, recv_sem,
):
    n = Net(send_sem, recv_sem)
    barrier, greetings = meet(n)

    def column_block(s):
        half = 1 - n.c if s < 4 else n.c
        return half * 4 + n.step("x", ORDER[s % 4])

    def w_copy(s):
        return pltpu.make_async_copy(
            window.at[:, pl.ds(pl.multiple_of(column_block(s) * 256, 256), 256)], w_stage.at[s], in_sem.at[s])

    w_copies = [w_copy(s) for s in range(8)]
    loads = [pltpu.make_async_copy(a, b, in_sem.at[8 + i]) for i, (a, b) in enumerate(
        ((co_test, ct_f), (range_test, rt_f), (core_right, cr_f), (core_left, cl_f)))]
    loads[0].start()
    for c in w_copies + loads[1:]:
        c.start()

    loads[0].wait()
    ct2[0:256, :], ct2[256:512, :] = split(ct_f[...])

    def co_block(s):
        w_copies[s].wait()
        block = column_block(s)
        cols = pl.ds(pl.multiple_of(block * 256, 256), 256)
        w_hi[:, cols], w_lo[:, cols] = split(w_stage[s])
        both = mm(ct2[...], w_hi[:, cols], NN)
        value = (both[:256] + both[256:]) + mm(ct2[0:256, :], w_lo[:, cols], NN)
        co[n.rows(block * 512, 256), :] = value[:, :128]
        co[n.rows(block * 512 + 256, 256), :] = value[:, 128:]
        return n.rows(block * 512, 512)

    core_copies = []
    for s in range(4):
        at = co_block(s)
        if s == 0:
            pl.semaphore_wait(barrier, greetings)
        core_copies.append(n.copy(co.at[at], co_core.at[s], n.partner))
    x_copies = []
    for s in range(4):
        at = co_block(4 + s)
        core_copies[s].wait_recv()
        co[at, :] = co[at, :] + co_core[s]
        if ORDER[s]:
            x_copies.append(n.copy(co.at[at], co_in.at[s], n.at(x=n.step("x", ORDER[s]))))
    co_own = (n.c * 4 + n.x) * 512

    loads[1].wait()
    rt_hi[...], rt_lo[...] = split(rt_f[...])
    y_copies = []
    for s in range(4):
        q = n.step("y", ORDER[s])
        rows = n.rows(q * 256, 256)
        value = mm3((w_hi[rows, :], w_lo[rows, :]), (rt_hi[...], rt_lo[...]), NN)
        rg[rows, :] = value
        rg_hi[rows, :], rg_lo[rows, :] = split(value)
        for flipped in (1, 0):
            if ORDER[s] or flipped:
                z, zl = (n.flip, 1 - n.zl) if flipped else (n.z, n.zl)
                y_copies.append(n.copy(rg.at[n.rows(q * 256 + zl * 128, 128)], rg_in.at[len(y_copies)], n.at(y=q, z=z)))

    loads[2].wait()
    cr_hi[...], cr_lo[...] = split(cr_f[...])

    def v_block(k):
        rows = n.rows(k * 256, 256)
        value = mm3((w_hi[rows, :], w_lo[rows, :]), (cr_hi[...], cr_lo[...]), NT)
        v_hi[rows, :], v_lo[rows, :] = split(value)

    pl.loop(0, 2)(v_block)
    total = co[n.rows(co_own, 512), :]
    for k, c in enumerate(x_copies):
        c.wait_recv()
        total = total + co_in[k]
    co[n.rows(co_own, 512), :] = total
    zh_peer = n.at(z=n.step("z", 2))
    co_z_copy = n.copy(co.at[n.rows(co_own + (1 - n.zh) * 256, 256)], co_z, zh_peer)
    pl.loop(2, 4)(v_block)

    y_own = n.rows(n.y * 256 + n.zl * 128, 128)
    total = rg[y_own, :]
    for k, c in enumerate(y_copies):
        c.wait_recv()
        total = total + rg_in[k]
    y_out[y_own, :] = total
    y_z_copy = n.copy(y_out.at[y_own], y_out.at[y_own], n.at(z=n.flip))
    part = split(total)
    gram[pl.ds(0, 256), :] = mm3(part, part, TN) * (1.0 / 16384)
    w_own = n.rows(co_own + n.zh * 256, 256)
    co_z_copy.wait_recv()
    total = co[w_own, :] + co_z[...]
    w_out[w_own, :] = total
    w_z_copy = n.copy(w_out.at[w_own], w_out.at[w_own], zh_peer)
    part = split(total)
    gram[pl.ds(256, 256), :] = mm3(part, part, NT) * (1.0 / 16384)
    reduce_g = Reduce(n, *PLANES[0], 16, gram, gram_out, g_core, g_plane, g_third)
    reduce_g.core_send()

    loads[3].wait()
    cl_hi[...], cl_lo[...] = split(cl_f[...])
    left = (cl_hi[...], cl_lo[...])
    cyw[pl.ds(0, 512), :] = mm3(left, (rg_hi[...], rg_lo[...]), NN)
    reduce_g.core_done()
    for k in range(2):
        cols = pl.ds(k * 256, 256)
        cyw[pl.ds(512 + 256 * k, 256), :] = mm3(
            (ct2[0:256, :], ct2[256:512, :]), (v_hi[:, cols], v_lo[:, cols]), NN)
    reduce_c = Reduce(n, *PLANES[1], 32, cyw, cyw_out, c_core, c_plane, c_third)
    reduce_c.core_send()
    for k in range(2):
        cols = pl.ds(k * 256, 256)
        zed[pl.ds(512 * k, 512), :] = mm3(left, (v_hi[:, cols], v_lo[:, cols]), NN)
        if k == 0:
            reduce_c.core_done()
    reduce_z = Reduce(n, *PLANES[2], 32, zed, z_out, z_core, z_plane, z_third)
    reduce_z.core_send()
    reduce_g.plane_done()
    reduce_z.core_done()

    y_z_copy.wait_recv()
    y_half = n.rows(n.y * 256, 256)
    y_gather = [n.copy(y_out.at[y_half], y_out.at[y_half], n.at(y=n.step("y", k))) for k in (2, 1, 3)]
    w_z_copy.wait_recv()
    w_half = n.rows(co_own, 512)
    w_gather = [n.copy(w_out.at[w_half], w_out.at[w_half], n.at(x=n.step("x", k))) for k in (2, 1, 3)]
    reduce_c.plane_done()
    reduce_g.third_done()
    reduce_z.plane_done()
    reduce_c.third_done()
    reduce_z.third_done()
    reduce_g.gathered()
    for c in w_gather:
        c.wait_recv()
    w_half = n.rows(n.c * 2048, 2048)
    w_core_copy = n.copy(w_out.at[w_half], w_out.at[w_half], n.partner)
    reduce_c.gathered()
    for c in y_gather:
        c.wait_recv()
    reduce_z.gathered()
    reduce_g.core_gathered()
    w_core_copy.wait_recv()
    reduce_c.core_gathered()
    reduce_z.core_gathered()
    for c in n.copies:
        c.wait_send()


def exchange(window, range_test, co_test, core_left, core_right):
    def f(*shape):
        return pltpu.VMEM(shape, F32)

    def b(*shape):
        return pltpu.VMEM(shape, BF16)

    def reduce_bufs(r):
        return [f(32 * r, 256), f(16 * r, 256), f(15, r, 256), f(4, r, 256)]

    scratch = [
        f(8, 1024, 256), b(1024, 2048), b(1024, 2048), f(2048, 256), f(256, 1024), f(512, 1024), f(512, 2048),
        b(2048, 256), b(2048, 256), b(512, 1024), b(512, 1024), b(512, 1024), b(512, 2048), b(512, 2048),
        f(4096, 128), f(4, 512, 128), f(3, 512, 128), f(256, 128),
        f(1024, 256), b(1024, 256), b(1024, 256), f(7, 128, 256), b(1024, 512), b(1024, 512),
        *reduce_bufs(16), *reduce_bufs(32), *reduce_bufs(32),
        pltpu.SemaphoreType.DMA((12,)), pltpu.SemaphoreType.DMA((COPIES,)), pltpu.SemaphoreType.DMA((COPIES,)),
    ]
    return pl.pallas_call(
        exchange_kernel,
        out_shape=[jax.ShapeDtypeStruct(s, F32) for s in (
            (1024, 256), (4096, 128), (512, 256), (1024, 256), (1024, 256))],
        in_specs=[pl.BlockSpec(memory_space=pl.ANY)] * 5,
        out_specs=[pl.BlockSpec(memory_space=pltpu.VMEM)] * 5,
        scratch_shapes=scratch,
        compiler_params=pltpu.CompilerParams(collective_id=0, has_side_effects=True, vmem_limit_bytes=67043328),
        name="exchange",
    )(window, range_test, co_test, core_left, core_right)


QUAD = 4


def factor_panel(tiles):
    lane = lax.broadcasted_iota(jnp.int32, (8, 128), 1)
    sub = lax.broadcasted_iota(jnp.int32, (8, 128), 0)
    group = (lane // 32) * 32
    p = list(tiles)
    e = [jnp.where(sub + 8 * t == lane - group, 1.0, 0.0).astype(F32) for t in range(4)]
    pivots = [None] * 32

    def row(x, s):
        return jnp.broadcast_to(x[s:s + 1, :], (8, 128))

    for j in range(0, 32, QUAD):
        t0 = j // 8
        cols = [[jnp.take_along_axis(p[t], group + (j + k), axis=1) for t in range(t0, 4)] for k in range(QUAD)]
        rows = [row(p[t0], j % 8 + k) for k in range(QUAD)]
        rows_e = [row(e[t0], j % 8 + k) for k in range(QUAD)]
        s = [[row(cols[k][0], j % 8 + l) for l in range(QUAD)] for k in range(QUAD)]
        coefs = []
        for k in range(QUAD):
            d = s[k][k]
            pivots[j + k] = d
            inv = 1.0 / d
            for l in range(k + 1, QUAD):
                f = s[k][l] * inv
                for m in range(l, QUAD):
                    s[l][m] = s[l][m] - s[k][m] * f
                cols[l] = [a - b * f for a, b in zip(cols[l], cols[k])]
                rows[l] = rows[l] - rows[k] * f
                rows_e[l] = rows_e[l] - rows_e[k] * f
            coefs.append(inv)
        for i, t in enumerate(range(t0, 4)):
            for k in range(QUAD):
                coef = cols[k][i] * coefs[k]
                if t == t0:
                    coef = jnp.where(sub > j % 8 + k, coef, 0.0)
                p[t] = p[t] - coef * rows[k]
                e[t] = e[t] - coef * rows_e[k]
    out = []
    for t in range(4):
        d = pivots[8 * t]
        for s in range(1, 8):
            d = jnp.where(sub == s, pivots[8 * t + s], d)
        out.append(e[t] * (1.0 / jnp.sqrt(d)))
    return out


def final_kernel(y_ref, w_ref, gram, cyw, zed, rb_ref, cb_ref, core_ref, mat):
    lane = lax.broadcasted_iota(jnp.int32, (32, 128), 1)
    eye = (lax.broadcasted_iota(jnp.int32, (256, 256), 0) == lax.broadcasted_iota(jnp.int32, (256, 256), 1)).astype(F32)
    mat[0, :, 0:256] = gram[pl.ds(0, 256), :]
    mat[1, :, 0:256] = gram[pl.ds(256, 256), :]
    cy = split(cyw[pl.ds(0, 512), :])
    mat[2, :, 0:256] = mm3(cy, cy, TN)
    cw = [split(cyw[pl.ds(512 + 256 * k, 256), :]) for k in range(2)]
    mat[3, :, 0:256] = mm3(cw[0], cw[0], NT) + mm3(cw[1], cw[1], NT)
    middle = sum(mm3(split(zed[pl.ds(512 * k, 512), :]), cw[k], NT) for k in range(2))
    inner = mm3(cy, split(middle), TN)
    for m in range(4):
        mat[m, :, 256:512] = eye
    for p in range(8):
        r0 = 32 * p
        c0 = r0 // 128 * 128
        packed = None
        for m in range(4):
            block = mat[m, r0:r0 + 32, c0:c0 + 128]
            shift = (m * 32 - r0 % 128) % 128
            if shift:
                block = pltpu.roll(block, shift, axis=1)
            packed = block if packed is None else jnp.where(lane // 32 == m, block, packed)
        inverse = jnp.concatenate(factor_panel([packed[8 * t:8 * t + 8, :] for t in range(4)]), axis=0)
        left = jnp.concatenate([jnp.where(lane // 32 == m, inverse, 0.0) for m in range(4)], axis=0)
        right = jnp.concatenate([mat[m, r0:r0 + 32, :] for m in range(4)], axis=0)
        upper = mmh(left, right, NN)
        for m in range(4):
            mat[m, r0:r0 + 32, :] = upper[32 * m:32 * m + 32, :]
        if p == 7:
            break
        b0 = (r0 + 32) // 128 * 128
        e1 = 256 + (r0 + 32 + 127) // 128 * 128
        for m in range(4):
            u = upper[32 * m:32 * m + 32, :]
            ut = u[:, b0:256].T[r0 + 32 - b0:, :]
            mat[m, r0 + 32:, b0:e1] = mat[m, r0 + 32:, b0:e1] - mmh(ut, u[:, b0:e1], NN)
    keep = lax.broadcasted_iota(jnp.int32, (256, 256), 0) <= lax.broadcasted_iota(jnp.int32, (256, 256), 1)
    y_inv = split(mat[0, :, 256:512])
    w_inv = split(mat[1, :, 256:512])
    for k in range(4):
        rb_ref[256 * k:256 * k + 256, :] = mm3(split(y_ref[256 * k:256 * k + 256, :]), y_inv, NT)
    for k in range(16):
        cb_ref[:, 128 * k:128 * k + 128] = mm3(w_inv, split(w_ref[256 * k:256 * k + 256, :]), NN)
    up_y = jnp.where(keep, mat[0, :, 0:256], 0.0)
    up_w = jnp.where(keep, mat[1, :, 0:256], 0.0)
    l_inv = mat[2, :, 256:512]
    r_inv = mat[3, :, 256:512]
    left = mmh(up_y, mmh(l_inv, l_inv, TN), NN)
    right = mmh(mmh(r_inv, r_inv, TN), up_w, NT)
    core_ref[...] = mmh(mmh(left, inner, NN), right, NN) * 16384.0


def final(*parts):
    return pl.pallas_call(
        final_kernel,
        out_shape=[jax.ShapeDtypeStruct(s, F32) for s in ((1024, 256), (256, 2048), (256, 256))],
        in_specs=[pl.BlockSpec(memory_space=pltpu.VMEM)] * 5,
        out_specs=[pl.BlockSpec(memory_space=pltpu.VMEM)] * 3,
        scratch_shapes=[pltpu.VMEM((4, 256, 512), F32)],
        compiler_params=pltpu.CompilerParams(vmem_limit_bytes=60000000),
        name="final",
    )(*parts)


def per_device(window, range_test, co_test, core_left, core_right):
    return tuple(final(*exchange(window, range_test, co_test, core_left, core_right)))


def solution(mesh):
    return jax.shard_map(
        per_device,
        mesh=mesh,
        in_specs=(P("cell", "tm"), P("tm", None), P(None, "cell"), P(None, "cell"), P(None, "tm")),
        out_specs=(P("cell", None), P(None, "tm"), P()),
        check_vma=False,
    )
```

```python
import functools
import math

import jax
import jax.numpy as jnp
from jax import lax
from jax.experimental import pallas as pl
from jax.experimental.pallas import tpu as pltpu
from jax.sharding import PartitionSpec as P

MESH = pl.DeviceIdType.MESH
F32 = jnp.float32
BF16 = jnp.bfloat16
NN = (((1,), (0,)), ((), ()))
NT = (((1,), (1,)), ((), ()))
TN = (((0,), (0,)), ((), ()))


def split(value):
    high = value.astype(BF16)
    low = (value - high.astype(F32)).astype(BF16)
    return high, low


def mm(left, right, dims):
    return lax.dot_general(left, right, dims, preferred_element_type=F32)


def mm3(left, right, dims):
    return mm(left[0], right[0], dims) + (mm(left[0], right[1], dims) + mm(left[1], right[0], dims))


def mm3f(left, right, dims):
    return mm3(split(left), split(right), dims)


def mmh(left, right, dims):
    return lax.dot_general(left, right, dims, precision=lax.Precision.HIGHEST, preferred_element_type=F32)


class Net:
    def __init__(self, send_sem, recv_sem):
        cell, tm = lax.axis_index("cell"), lax.axis_index("tm")
        self.x, self.zh, self.c = cell // 4, lax.rem(cell // 2, 2), lax.rem(cell, 2)
        self.y, self.zl = tm // 2, lax.rem(tm, 2)
        self.z = self.zh * 2 + self.zl
        self.flip = self.zh * 2 + 1 - self.zl
        self.partner = self.at(c=1 - self.c)
        self.send_sem, self.recv_sem = send_sem, recv_sem
        self.copies = []

    def at(self, x=None, y=None, z=None, c=None):
        x = self.x if x is None else x
        y = self.y if y is None else y
        c = self.c if c is None else c
        zh, zl = (self.zh, self.zl) if z is None else (z // 2, lax.rem(z, 2))
        return ((x * 2 + zh) * 2 + c, y * 2 + zl)

    def step(self, axis, k):
        return getattr(self, axis) if k == 0 else lax.rem(getattr(self, axis) + k, 4)

    def rows(self, start, size):
        return pl.ds(pl.multiple_of(start, 8), size)

    def copy(self, src, dst, device):
        k = len(self.copies)
        c = pltpu.make_async_remote_copy(
            src_ref=src, dst_ref=dst, send_sem=self.send_sem.at[k], recv_sem=self.recv_sem.at[k],
            device_id=device, device_id_type=MESH,
        )
        c.start()
        self.copies.append(c)
        return c


class Reduce:
    def __init__(self, net, axes, rows, source, out, core_in, first_in, second_in, third_in):
        self.net, self.axes, self.r = net, axes, rows
        self.source, self.out = source, out
        self.core_in, self.first_in, self.second_in, self.third_in = core_in, first_in, second_in, third_in

    def place(self, i=0, j=0):
        n, (a, b, _) = self.net, self.axes
        return n.c * 16 * self.r + (n.step(a, i) * 4 + n.step(b, j)) * self.r

    def block(self, i=0):
        n = self.net
        return n.rows(n.c * 16 * self.r + n.step(self.axes[0], i) * 4 * self.r, 4 * self.r)

    def peer(self, axis, k):
        return self.net.at(**{axis: self.net.step(axis, k)})

    def core_send(self):
        n, half = self.net, 16 * self.r
        self.c = n.copy(self.source.at[n.rows((1 - n.c) * half, half)], self.core_in, n.partner)

    def core_done(self):
        n, r = self.net, self.r
        self.c.wait_recv()
        own = n.rows(n.c * 16 * r, 16 * r)
        self.source[own, :] = self.source[own, :] + self.core_in[...]
        self.f = [n.copy(self.source.at[self.block(k)], self.first_in.at[i], self.peer(self.axes[0], k))
                  for i, k in enumerate((2, 1, 3))]

    def first_done(self):
        n, r = self.net, self.r
        for c in self.f:
            c.wait_recv()
        own = self.block()
        self.source[own, :] = (self.source[own, :] + self.first_in[0]) + (self.first_in[1] + self.first_in[2])
        self.s = [n.copy(self.source.at[n.rows(self.place(0, k), r)], self.second_in.at[i], self.peer(self.axes[1], k))
                  for i, k in enumerate((2, 1, 3))]

    def second_done(self):
        n, r = self.net, self.r
        for c in self.s:
            c.wait_recv()
        own = n.rows(self.place(), r)
        me = getattr(n, self.axes[2])
        self.third_in[me] = (self.source[own, :] + self.second_in[0]) + (self.second_in[1] + self.second_in[2])
        self.t = [n.copy(self.third_in.at[me], self.third_in.at[me], self.peer(self.axes[2], k)) for k in (2, 1, 3)]

    def third_done(self):
        n, r = self.net, self.r
        for c in self.t:
            c.wait_recv()
        own = n.rows(self.place(), r)
        self.out[own, :] = (self.third_in[0] + self.third_in[1]) + (self.third_in[2] + self.third_in[3])
        self.g = [n.copy(self.out.at[own], self.out.at[own], self.peer(self.axes[1], k)) for k in (2, 1, 3)]

    def second_gathered(self):
        n = self.net
        for c in self.g:
            c.wait_recv()
        own = self.block()
        self.h = [n.copy(self.out.at[own], self.out.at[own], self.peer(self.axes[0], k)) for k in (2, 1, 3)]

    def gathered(self):
        n, half = self.net, 16 * self.r
        for c in self.h:
            c.wait_recv()
        own = n.rows(n.c * half, half)
        self.c2 = n.copy(self.out.at[own], self.out.at[own], n.partner)

    def core_gathered(self):
        self.c2.wait_recv()


COPIES = 100
ORDER = (2, 1, 3, 0)
AXES = (("y", "x", "z"), ("z", "x", "y"), ("z", "y", "x"))


def meet(n):
    barrier = pltpu.get_barrier_semaphore()
    peers = [n.partner]
    for axis in "xyz":
        peers += [n.at(**{axis: n.step(axis, k)}) for k in (1, 2, 3)]
    peers += [n.at(y=n.step("y", k), z=n.flip) for k in (1, 2, 3)]
    for peer in peers:
        pl.semaphore_signal(barrier, inc=1, device_id=peer, device_id_type=MESH)
    return barrier, len(peers)


def exchange_kernel(
    window, range_test, co_test, core_left, core_right,
    y_out, w_out, gram_out, cyw_out, z_out,
    w_stage, w_hi, w_lo, rt_f, ct_f, cl_f, cr_f, rt_hi, rt_lo, ct2, cl_hi, cl_lo, cr_hi, cr_lo,
    co, co_core, co_in, co_z, rg, rg_hi, rg_lo, rg_in, v_hi, v_lo,
    gram, g_core, g_first, g_second, g_third, cyw, c_core, c_first, c_second, c_third, zed, z_core, z_first, z_second, z_third,
    in_sem, send_sem, recv_sem,
):
    n = Net(send_sem, recv_sem)
    barrier, greetings = meet(n)

    def column_block(s):
        half = 1 - n.c if s < 4 else n.c
        return half * 4 + n.step("x", ORDER[s % 4])

    def w_copy(s):
        return pltpu.make_async_copy(
            window.at[:, pl.ds(pl.multiple_of(column_block(s) * 256, 256), 256)], w_stage.at[s], in_sem.at[s])

    w_copies = [w_copy(s) for s in range(8)]
    loads = [pltpu.make_async_copy(a, b, in_sem.at[8 + i]) for i, (a, b) in enumerate(
        ((co_test, ct_f), (range_test, rt_f), (core_right, cr_f), (core_left, cl_f)))]
    loads[0].start()
    for c in w_copies + loads[1:]:
        c.start()

    loads[0].wait()
    ct2[0:256, :], ct2[256:512, :] = split(ct_f[...])

    def co_block(s):
        w_copies[s].wait()
        block = column_block(s)
        cols = pl.ds(pl.multiple_of(block * 256, 256), 256)
        w_hi[:, cols], w_lo[:, cols] = split(w_stage[s])
        both = mm(ct2[...], w_hi[:, cols], NN)
        value = (both[:256] + both[256:]) + mm(ct2[0:256, :], w_lo[:, cols], NN)
        co[n.rows(block * 512, 256), :] = value[:, :128]
        co[n.rows(block * 512 + 256, 256), :] = value[:, 128:]
        return n.rows(block * 512, 512)

    core_copies = []
    for s in range(4):
        at = co_block(s)
        if s == 0:
            pl.semaphore_wait(barrier, greetings)
        core_copies.append(n.copy(co.at[at], co_core.at[s], n.partner))
    x_copies = []
    for s in range(4):
        at = co_block(4 + s)
        core_copies[s].wait_recv()
        co[at, :] = co[at, :] + co_core[s]
        if ORDER[s]:
            x_copies.append(n.copy(co.at[at], co_in.at[s], n.at(x=n.step("x", ORDER[s]))))
    co_own = (n.c * 4 + n.x) * 512

    loads[1].wait()
    rt_hi[...], rt_lo[...] = split(rt_f[...])
    y_copies = []
    for s in range(4):
        q = n.step("y", ORDER[s])
        rows = n.rows(q * 256, 256)
        value = mm3((w_hi[rows, :], w_lo[rows, :]), (rt_hi[...], rt_lo[...]), NN)
        rg[rows, :] = value
        rg_hi[rows, :], rg_lo[rows, :] = split(value)
        for flipped in (1, 0):
            if ORDER[s] or flipped:
                z, zl = (n.flip, 1 - n.zl) if flipped else (n.z, n.zl)
                y_copies.append(n.copy(rg.at[n.rows(q * 256 + zl * 128, 128)], rg_in.at[len(y_copies)], n.at(y=q, z=z)))

    loads[2].wait()
    cr_hi[...], cr_lo[...] = split(cr_f[...])

    def v_block(k):
        rows = n.rows(k * 256, 256)
        value = mm3((w_hi[rows, :], w_lo[rows, :]), (cr_hi[...], cr_lo[...]), NT)
        v_hi[rows, :], v_lo[rows, :] = split(value)

    pl.loop(0, 2)(v_block)
    total = co[n.rows(co_own, 512), :]
    for k, c in enumerate(x_copies):
        c.wait_recv()
        total = total + co_in[k]
    co[n.rows(co_own, 512), :] = total
    zh_peer = n.at(z=n.step("z", 2))
    co_z_copy = n.copy(co.at[n.rows(co_own + (1 - n.zh) * 256, 256)], co_z, zh_peer)
    pl.loop(2, 4)(v_block)

    y_own = n.rows(n.y * 256 + n.zl * 128, 128)
    total = rg[y_own, :]
    for k, c in enumerate(y_copies):
        c.wait_recv()
        total = total + rg_in[k]
    y_out[y_own, :] = total
    y_z_copy = n.copy(y_out.at[y_own], y_out.at[y_own], n.at(z=n.flip))
    part = split(total)
    gram[pl.ds(0, 256), :] = mm3(part, part, TN) * (1.0 / 16384)
    w_own = n.rows(co_own + n.zh * 256, 256)
    co_z_copy.wait_recv()
    total = co[w_own, :] + co_z[...]
    w_out[w_own, :] = total
    w_z_copy = n.copy(w_out.at[w_own], w_out.at[w_own], zh_peer)
    part = split(total)
    gram[pl.ds(256, 256), :] = mm3(part, part, NT) * (1.0 / 16384)
    reduce_g = Reduce(n, AXES[0], 16, gram, gram_out, g_core, g_first, g_second, g_third)
    reduce_g.core_send()

    loads[3].wait()
    cl_hi[...], cl_lo[...] = split(cl_f[...])
    left = (cl_hi[...], cl_lo[...])
    cyw[pl.ds(0, 512), :] = mm3(left, (rg_hi[...], rg_lo[...]), NN)
    reduce_g.core_done()
    for k in range(2):
        cols = pl.ds(k * 256, 256)
        cyw[pl.ds(512 + 256 * k, 256), :] = mm3(
            (ct2[0:256, :], ct2[256:512, :]), (v_hi[:, cols], v_lo[:, cols]), NN)
    reduce_c = Reduce(n, AXES[1], 32, cyw, cyw_out, c_core, c_first, c_second, c_third)
    reduce_c.core_send()
    for k in range(2):
        cols = pl.ds(k * 256, 256)
        zed[pl.ds(512 * k, 512), :] = mm3(left, (v_hi[:, cols], v_lo[:, cols]), NN)
        if k == 0:
            reduce_c.core_done()
    reduce_z = Reduce(n, AXES[2], 32, zed, z_out, z_core, z_first, z_second, z_third)
    reduce_z.core_send()
    reduce_g.first_done()
    reduce_z.core_done()
    y_z_copy.wait_recv()
    y_half = n.rows(n.y * 256, 256)
    y_gather = [n.copy(y_out.at[y_half], y_out.at[y_half], n.at(y=n.step("y", k))) for k in (2, 1, 3)]
    w_z_copy.wait_recv()
    w_half = n.rows(co_own, 512)
    w_gather = [n.copy(w_out.at[w_half], w_out.at[w_half], n.at(x=n.step("x", k))) for k in (2, 1, 3)]
    reduce_g.second_done()
    reduce_c.first_done()
    reduce_g.third_done()
    reduce_z.first_done()
    reduce_c.second_done()
    reduce_g.second_gathered()
    reduce_c.third_done()
    reduce_z.second_done()
    reduce_g.gathered()
    reduce_c.second_gathered()
    reduce_z.third_done()
    for c in w_gather:
        c.wait_recv()
    w_half = n.rows(n.c * 2048, 2048)
    w_core_copy = n.copy(w_out.at[w_half], w_out.at[w_half], n.partner)
    reduce_z.second_gathered()
    reduce_c.gathered()
    for c in y_gather:
        c.wait_recv()
    reduce_z.gathered()
    reduce_g.core_gathered()
    w_core_copy.wait_recv()
    reduce_c.core_gathered()
    reduce_z.core_gathered()
    for c in n.copies:
        c.wait_send()


def exchange(window, range_test, co_test, core_left, core_right):
    def f(*shape):
        return pltpu.VMEM(shape, F32)

    def b(*shape):
        return pltpu.VMEM(shape, BF16)

    def reduce_bufs(r):
        return [f(32 * r, 256), f(16 * r, 256), f(3, 4 * r, 256), f(3, r, 256), f(4, r, 256)]

    scratch = [
        f(8, 1024, 256), b(1024, 2048), b(1024, 2048), f(2048, 256), f(256, 1024), f(512, 1024), f(512, 2048),
        b(2048, 256), b(2048, 256), b(512, 1024), b(512, 1024), b(512, 1024), b(512, 2048), b(512, 2048),
        f(4096, 128), f(4, 512, 128), f(3, 512, 128), f(256, 128),
        f(1024, 256), b(1024, 256), b(1024, 256), f(7, 128, 256), b(1024, 512), b(1024, 512),
        *reduce_bufs(16), *reduce_bufs(32), *reduce_bufs(32),
        pltpu.SemaphoreType.DMA((12,)), pltpu.SemaphoreType.DMA((COPIES,)), pltpu.SemaphoreType.DMA((COPIES,)),
    ]
    return pl.pallas_call(
        exchange_kernel,
        out_shape=[jax.ShapeDtypeStruct(s, F32) for s in (
            (1024, 256), (4096, 128), (512, 256), (1024, 256), (1024, 256))],
        in_specs=[pl.BlockSpec(memory_space=pl.ANY)] * 5,
        out_specs=[pl.BlockSpec(memory_space=pltpu.VMEM)] * 5,
        scratch_shapes=scratch,
        compiler_params=pltpu.CompilerParams(collective_id=0, has_side_effects=True, vmem_limit_bytes=67043328),
        name="exchange",
    )(window, range_test, co_test, core_left, core_right)


QUAD = 8


def factor_panel(tiles):
    lane = lax.broadcasted_iota(jnp.int32, (8, 128), 1)
    sub = lax.broadcasted_iota(jnp.int32, (8, 128), 0)
    group = (lane // 32) * 32
    p = list(tiles)
    e = [jnp.where(sub + 8 * t == lane - group, 1.0, 0.0).astype(F32) for t in range(4)]
    pivots = [None] * 32

    def row(x, s):
        return jnp.broadcast_to(x[s:s + 1, :], (8, 128))

    for j in range(0, 32, QUAD):
        t0 = j // 8
        cols = [[jnp.take_along_axis(p[t], group + (j + k), axis=1) for t in range(t0, 4)] for k in range(QUAD)]
        rows = [row(p[t0], j % 8 + k) for k in range(QUAD)]
        rows_e = [row(e[t0], j % 8 + k) for k in range(QUAD)]
        s = [[row(cols[k][0], j % 8 + l) for l in range(QUAD)] for k in range(QUAD)]
        coefs = []
        for k in range(QUAD):
            d = s[k][k]
            pivots[j + k] = d
            inv = 1.0 / d
            for l in range(k + 1, QUAD):
                f = s[k][l] * inv
                for m in range(l, QUAD):
                    s[l][m] = s[l][m] - s[k][m] * f
                cols[l] = [a - b * f for a, b in zip(cols[l], cols[k])]
                rows[l] = rows[l] - rows[k] * f
                rows_e[l] = rows_e[l] - rows_e[k] * f
            coefs.append(inv)
        for i, t in enumerate(range(t0, 4)):
            for k in range(QUAD):
                coef = cols[k][i] * coefs[k]
                if t == t0:
                    coef = jnp.where(sub > j % 8 + k, coef, 0.0)
                p[t] = p[t] - coef * rows[k]
                e[t] = e[t] - coef * rows_e[k]
    out = []
    for t in range(4):
        d = pivots[8 * t]
        for s in range(1, 8):
            d = jnp.where(sub == s, pivots[8 * t + s], d)
        out.append(e[t] * (1.0 / jnp.sqrt(d)))
    return out


def stacked(left, right):
    both = mm(jnp.concatenate(left, axis=1), jnp.concatenate([right[0], right[0]], axis=0), NN)
    return both + mm(left[0], right[1], NN)


def final_kernel(
    y_hbm, w_hbm, gram, cyw, zed, rb_hbm, cb_hbm, core_ref, mat, y_ref, w_ref, rb_ref, cb_ref, mid, in_sem, out_sem
):
    loads = [pltpu.make_async_copy(y_hbm, y_ref, in_sem.at[0]), pltpu.make_async_copy(w_hbm, w_ref, in_sem.at[1])]
    for c in loads:
        c.start()
    lane = lax.broadcasted_iota(jnp.int32, (32, 128), 1)
    eye = (lax.broadcasted_iota(jnp.int32, (256, 256), 0) == lax.broadcasted_iota(jnp.int32, (256, 256), 1)).astype(F32)
    mat[0, :, 0:256] = gram[pl.ds(0, 256), :]
    mat[1, :, 0:256] = gram[pl.ds(256, 256), :]
    cy = split(cyw[pl.ds(0, 512), :])
    mat[2, :, 0:256] = mm3(cy, cy, TN)
    cw = [split(cyw[pl.ds(512 + 256 * k, 256), :]) for k in range(2)]
    mat[3, :, 0:256] = mm3(cw[0], cw[0], NT) + mm3(cw[1], cw[1], NT)
    for m in range(4):
        mat[m, :, 256:512] = eye
    for p in range(8):
        r0 = 32 * p
        c0 = r0 // 128 * 128
        e1 = 256 + (r0 + 32 + 127) // 128 * 128
        rows = slice(64 * p, 64 * p + 64)
        mid[rows, :] = (mm3(split(zed[64 * p:64 * p + 64, :]), cw[0], NT)
                        + mm3(split(zed[512 + 64 * p:512 + 64 * p + 64, :]), cw[1], NT))
        packed = None
        for m in range(4):
            block = mat[m, r0:r0 + 32, c0:c0 + 128]
            shift = (m * 32 - r0 % 128) % 128
            if shift:
                block = pltpu.roll(block, shift, axis=1)
            packed = block if packed is None else jnp.where(lane // 32 == m, block, packed)
        inverse = jnp.concatenate(factor_panel([packed[8 * t:8 * t + 8, :] for t in range(4)]), axis=0)
        left = jnp.concatenate([jnp.where(lane // 32 == m, inverse, 0.0) for m in range(4)], axis=0)
        right = jnp.concatenate([mat[m, r0:r0 + 32, c0:e1] for m in range(4)], axis=0)
        upper = stacked(split(left), split(right))
        for m in range(4):
            mat[m, r0:r0 + 32, c0:e1] = upper[32 * m:32 * m + 32, :]
        if p == 7:
            break
        b0 = (r0 + 32) // 128 * 128
        u_high, u_low = split(upper[:, b0 - c0:])
        below = split(upper[:, b0 - c0:256 - c0].T[r0 + 32 - b0:, :])
        zero = jnp.zeros((32, e1 - b0), BF16)
        for m in range(4):
            mine = [jnp.concatenate([u[32 * m:32 * m + 32] if k == m else zero for k in range(4)], axis=0)
                    for u in (u_high, u_low)]
            mat[m, r0 + 32:, b0:e1] = mat[m, r0 + 32:, b0:e1] - stacked(below, mine)
    keep = lax.broadcasted_iota(jnp.int32, (256, 256), 0) <= lax.broadcasted_iota(jnp.int32, (256, 256), 1)
    y_inv = split(mat[0, :, 256:512])
    w_inv = split(mat[1, :, 256:512])
    for c in loads:
        c.wait()
    stores = []
    for k in range(2):
        rows = slice(512 * k, 512 * k + 512)
        rb_ref[rows, :] = mm3(split(y_ref[rows, :]), y_inv, NT)
        stores.append(pltpu.make_async_copy(rb_ref.at[rows], rb_hbm.at[rows], out_sem.at[k]))
        stores[-1].start()
    for k in range(8):
        cols = slice(256 * k, 256 * k + 256)
        block = jnp.concatenate([w_ref[512 * k:512 * k + 256, :], w_ref[512 * k + 256:512 * k + 512, :]], axis=1)
        cb_ref[:, cols] = mm3(w_inv, split(block), NN)
        stores.append(pltpu.make_async_copy(cb_ref.at[:, cols], cb_hbm.at[:, cols], out_sem.at[2 + k]))
        stores[-1].start()
    up_y = jnp.where(keep, mat[0, :, 0:256], 0.0)
    up_w = jnp.where(keep, mat[1, :, 0:256], 0.0)
    l_inv = split(mat[2, :, 256:512])
    r_inv = split(mat[3, :, 256:512])
    inner = mm3(cy, split(mid[...]), TN)
    left = mm3f(up_y, mm3(l_inv, l_inv, TN), NN)
    right = mm3f(mm3(r_inv, r_inv, TN), up_w, NT)
    core_ref[...] = mm3f(mm3f(left, inner, NN), right, NN) * 16384.0
    for c in stores:
        c.wait()


def final(*parts):
    spec, hbm = pl.BlockSpec(memory_space=pltpu.VMEM), pl.BlockSpec(memory_space=pl.ANY)
    return pl.pallas_call(
        final_kernel,
        out_shape=[jax.ShapeDtypeStruct(s, F32) for s in ((1024, 256), (256, 2048), (256, 256))],
        in_specs=[hbm, hbm, spec, spec, spec],
        out_specs=[hbm, hbm, spec],
        scratch_shapes=[pltpu.VMEM(s, F32) for s in (
            (4, 256, 512), (1024, 256), (4096, 128), (1024, 256), (256, 2048), (512, 256))]
        + [pltpu.SemaphoreType.DMA((2,)), pltpu.SemaphoreType.DMA((10,))],
        compiler_params=pltpu.CompilerParams(vmem_limit_bytes=67043328),
        name="final",
    )(*parts)


def per_device(window, range_test, co_test, core_left, core_right):
    return tuple(final(*exchange(window, range_test, co_test, core_left, core_right)))


def solution(mesh):
    return jax.shard_map(
        per_device,
        mesh=mesh,
        in_specs=(P("cell", "tm"), P("tm", None), P(None, "cell"), P(None, "cell"), P(None, "tm")),
        out_specs=(P("cell", None), P(None, "tm"), P()),
        check_vma=False,
    )
```

```python
import functools
import math

import jax
import jax.numpy as jnp
from jax import lax
from jax.experimental import pallas as pl
from jax.experimental.pallas import tpu as pltpu
from jax.sharding import PartitionSpec as P

MESH = pl.DeviceIdType.MESH
F32 = jnp.float32
BF16 = jnp.bfloat16
NN = (((1,), (0,)), ((), ()))
NT = (((1,), (1,)), ((), ()))
TN = (((0,), (0,)), ((), ()))


def split(value):
    high = value.astype(BF16)
    low = (value - high.astype(F32)).astype(BF16)
    return high, low


def mm(left, right, dims):
    return lax.dot_general(left, right, dims, preferred_element_type=F32)


def mm3(left, right, dims):
    return mm(left[0], right[0], dims) + (mm(left[0], right[1], dims) + mm(left[1], right[0], dims))


def mm3f(left, right, dims):
    return mm3(split(left), split(right), dims)


def mmh(left, right, dims):
    return lax.dot_general(left, right, dims, precision=lax.Precision.HIGHEST, preferred_element_type=F32)


class Net:
    def __init__(self, send_sem, recv_sem):
        cell, tm = lax.axis_index("cell"), lax.axis_index("tm")
        self.x, self.zh, self.c = cell // 4, lax.rem(cell // 2, 2), lax.rem(cell, 2)
        self.y, self.zl = tm // 2, lax.rem(tm, 2)
        self.z = self.zh * 2 + self.zl
        self.flip = self.zh * 2 + 1 - self.zl
        self.partner = self.at(c=1 - self.c)
        self.send_sem, self.recv_sem = send_sem, recv_sem
        self.copies = []

    def at(self, x=None, y=None, z=None, c=None):
        x = self.x if x is None else x
        y = self.y if y is None else y
        c = self.c if c is None else c
        zh, zl = (self.zh, self.zl) if z is None else (z // 2, lax.rem(z, 2))
        return ((x * 2 + zh) * 2 + c, y * 2 + zl)

    def step(self, axis, k):
        return getattr(self, axis) if k == 0 else lax.rem(getattr(self, axis) + k, 4)

    def rows(self, start, size):
        return pl.ds(pl.multiple_of(start, 8), size)

    def copy(self, src, dst, device):
        k = len(self.copies)
        c = pltpu.make_async_remote_copy(
            src_ref=src, dst_ref=dst, send_sem=self.send_sem.at[k], recv_sem=self.recv_sem.at[k],
            device_id=device, device_id_type=MESH,
        )
        c.start()
        self.copies.append(c)
        return c


class Reduce:
    def __init__(self, net, axes, rows, source, out, core_in, first_in, second_in, third_in):
        self.net, self.axes, self.r = net, axes, rows
        self.source, self.out = source, out
        self.core_in, self.first_in, self.second_in, self.third_in = core_in, first_in, second_in, third_in

    def place(self, i=0, j=0):
        n, (a, b, _) = self.net, self.axes
        return n.c * 16 * self.r + (n.step(a, i) * 4 + n.step(b, j)) * self.r

    def block(self, i=0):
        n = self.net
        return n.rows(n.c * 16 * self.r + n.step(self.axes[0], i) * 4 * self.r, 4 * self.r)

    def peer(self, axis, k):
        return self.net.at(**{axis: self.net.step(axis, k)})

    def core_send(self):
        n, half = self.net, 16 * self.r
        self.c = n.copy(self.source.at[n.rows((1 - n.c) * half, half)], self.core_in, n.partner)

    def core_done(self):
        n, r = self.net, self.r
        self.c.wait_recv()
        own = n.rows(n.c * 16 * r, 16 * r)
        self.source[own, :] = self.source[own, :] + self.core_in[...]
        self.f = [n.copy(self.source.at[self.block(k)], self.first_in.at[i], self.peer(self.axes[0], k))
                  for i, k in enumerate((2, 1, 3))]

    def first_done(self):
        n, r = self.net, self.r
        for c in self.f:
            c.wait_recv()
        own = self.block()
        self.source[own, :] = (self.source[own, :] + self.first_in[0]) + (self.first_in[1] + self.first_in[2])
        self.s = [n.copy(self.source.at[n.rows(self.place(0, k), r)], self.second_in.at[i], self.peer(self.axes[1], k))
                  for i, k in enumerate((2, 1, 3))]

    def second_done(self):
        n, r = self.net, self.r
        for c in self.s:
            c.wait_recv()
        own = n.rows(self.place(), r)
        me = getattr(n, self.axes[2])
        self.third_in[me] = (self.source[own, :] + self.second_in[0]) + (self.second_in[1] + self.second_in[2])
        self.t = [n.copy(self.third_in.at[me], self.third_in.at[me], self.peer(self.axes[2], k)) for k in (2, 1, 3)]

    def third_done(self):
        n, r = self.net, self.r
        for c in self.t:
            c.wait_recv()
        own = n.rows(self.place(), r)
        self.out[own, :] = (self.third_in[0] + self.third_in[1]) + (self.third_in[2] + self.third_in[3])
        self.g = [n.copy(self.out.at[own], self.out.at[own], self.peer(self.axes[1], k)) for k in (2, 1, 3)]

    def second_gathered(self):
        n = self.net
        for c in self.g:
            c.wait_recv()
        own = self.block()
        self.h = [n.copy(self.out.at[own], self.out.at[own], self.peer(self.axes[0], k)) for k in (2, 1, 3)]

    def gathered(self):
        n, half = self.net, 16 * self.r
        for c in self.h:
            c.wait_recv()
        own = n.rows(n.c * half, half)
        self.c2 = n.copy(self.out.at[own], self.out.at[own], n.partner)

    def core_gathered(self):
        self.c2.wait_recv()


COPIES = 100
ORDER = (2, 1, 3, 0)
AXES = (("y", "x", "z"), ("x", "y", "z"), ("z", "y", "x"))


def meet(n):
    barrier = pltpu.get_barrier_semaphore()
    peers = [n.partner]
    for axis in "xyz":
        peers += [n.at(**{axis: n.step(axis, k)}) for k in (1, 2, 3)]
    peers += [n.at(x=n.step("x", k), z=n.step("z", 2)) for k in (1, 2, 3)]
    for peer in peers:
        pl.semaphore_signal(barrier, inc=1, device_id=peer, device_id_type=MESH)
    return barrier, len(peers)


def exchange_kernel(
    window, range_test, co_test, core_left, core_right,
    y_out, w_out, gram_out, cyw_out, z_out,
    w_stage, w_hi, w_lo, rt_f, ct_f, cl_f, cr_f, rt_hi, rt_lo, ct2, cl_hi, cl_lo, cr_hi, cr_lo,
    co, co_core, co_in, rg, rg_hi, rg_lo, rg_in, rg_z, v_hi, v_lo,
    gram, g_core, g_first, g_second, g_third, cyw, c_core, c_first, c_second, c_third, zed, z_core, z_first, z_second, z_third,
    in_sem, send_sem, recv_sem,
):
    n = Net(send_sem, recv_sem)
    barrier, greetings = meet(n)

    rows_of = [n.rows(n.step("y", k) * 256, 256) for k in ORDER]
    w_copies = [pltpu.make_async_copy(window.at[rows_of[s]], w_stage.at[s], in_sem.at[s]) for s in range(4)]
    loads = [pltpu.make_async_copy(a, b, in_sem.at[4 + i]) for i, (a, b) in enumerate(
        ((range_test, rt_f), (co_test, ct_f), (core_right, cr_f), (core_left, cl_f)))]
    loads[0].start()
    for c in w_copies[:2]:
        c.start()

    def split_rows(s):
        w_copies[s].wait()
        w_hi[rows_of[s], :], w_lo[rows_of[s], :] = split(w_stage[s])

    def range_block(s):
        rows = rows_of[s]
        value = mm3((w_hi[rows, :], w_lo[rows, :]), (rt_hi[...], rt_lo[...]), NN)
        rg[rows, :] = value
        rg_hi[rows, :], rg_lo[rows, :] = split(value)

    loads[0].wait()
    rt_hi[...], rt_lo[...] = split(rt_f[...])
    for c in w_copies[2:] + loads[1:2]:
        c.start()
    y_copies = []
    for s in range(3):
        split_rows(s)
        range_block(s)
        if s == 0:
            pl.semaphore_wait(barrier, greetings)
            loads[2].start()
        y_copies.append(n.copy(rg.at[rows_of[s]], rg_in.at[s], n.at(y=n.step("y", ORDER[s]))))
    loads[3].start()
    split_rows(3)

    loads[1].wait()
    ct2[0:256, :], ct2[256:512, :] = split(ct_f[...])

    def co_block(half, k):
        block = half * 4 + n.step("x", k)
        cols = pl.ds(pl.multiple_of(block * 256, 256), 256)
        both = mm(ct2[...], w_hi[:, cols], NN)
        value = (both[:256] + both[256:]) + mm(ct2[0:256, :], w_lo[:, cols], NN)
        co[n.rows(block * 512, 256), :] = value[:, :128]
        co[n.rows(block * 512 + 256, 256), :] = value[:, 128:]
        return n.rows(block * 512, 512)

    core_copies = []
    for s in range(4):
        at = co_block(1 - n.c, ORDER[s])
        core_copies.append(n.copy(co.at[at], co_core.at[s], n.partner))
    x_copies = []
    zh_far, z_far = 1 - n.zh, n.step("z", 2)
    for s in range(4):
        at = co_block(n.c, ORDER[s])
        core_copies[s].wait_recv()
        co[at, :] = co[at, :] + co_core[s]
        x = n.step("x", ORDER[s])
        base = (n.c * 4 + x) * 512
        x_copies.append(n.copy(co.at[n.rows(base + zh_far * 256, 256)], co_in.at[len(x_copies)], n.at(x=x, z=z_far)))
        if ORDER[s]:
            x_copies.append(n.copy(co.at[n.rows(base + n.zh * 256, 256)], co_in.at[len(x_copies)], n.at(x=x)))
    co_own = (n.c * 4 + n.x) * 512
    range_block(3)

    loads[2].wait()
    cr_hi[...], cr_lo[...] = split(cr_f[...])

    def v_block(k):
        rows = n.rows(k * 256, 256)
        value = mm3((w_hi[rows, :], w_lo[rows, :]), (cr_hi[...], cr_lo[...]), NT)
        v_hi[rows, :], v_lo[rows, :] = split(value)

    pl.loop(0, 3)(v_block)
    y_half = rows_of[3]
    total = rg[y_half, :]
    for k, c in enumerate(y_copies):
        c.wait_recv()
        total = total + rg_in[k]
    rg[y_half, :] = total
    z_flip = n.at(z=n.flip)
    rg_z_copy = n.copy(rg.at[n.rows(n.y * 256 + (1 - n.zl) * 128, 128)], rg_z, z_flip)
    pl.loop(3, 4)(v_block)

    loads[3].wait()
    cl_hi[...], cl_lo[...] = split(cl_f[...])
    left = (cl_hi[...], cl_lo[...])
    zed[pl.ds(0, 512), :] = mm3(left, (v_hi[:, 0:256], v_lo[:, 0:256]), NN)
    zed[pl.ds(512, 512), :] = mm3(left, (v_hi[:, 256:512], v_lo[:, 256:512]), NN)
    reduce_z = Reduce(n, AXES[2], 32, zed, z_out, z_core, z_first, z_second, z_third)
    reduce_z.core_send()
    cyw[pl.ds(0, 512), :] = mm3(left, (rg_hi[...], rg_lo[...]), NN)
    reduce_z.core_done()
    for k in range(2):
        cols = pl.ds(k * 256, 256)
        cyw[pl.ds(512 + 256 * k, 256), :] = mm3(
            (ct2[0:256, :], ct2[256:512, :]), (v_hi[:, cols], v_lo[:, cols]), NN)
    reduce_c = Reduce(n, AXES[1], 32, cyw, cyw_out, c_core, c_first, c_second, c_third)
    reduce_c.core_send()
    y_own = n.rows(n.y * 256 + n.zl * 128, 128)
    rg_z_copy.wait_recv()
    total = rg[y_own, :] + rg_z[...]
    y_out[y_own, :] = total
    part = split(total)
    gram[pl.ds(0, 256), :] = mm3(part, part, TN) * (1.0 / 16384)
    reduce_c.core_done()
    w_own = n.rows(co_own + n.zh * 256, 256)
    total = co[w_own, :]
    for k, c in enumerate(x_copies):
        c.wait_recv()
        total = total + co_in[k]
    w_out[w_own, :] = total
    part = split(total)
    gram[pl.ds(256, 256), :] = mm3(part, part, NT) * (1.0 / 16384)
    reduce_g = Reduce(n, AXES[0], 16, gram, gram_out, g_core, g_first, g_second, g_third)
    reduce_g.core_send()
    y_z_copy = n.copy(y_out.at[y_own], y_out.at[y_own], z_flip)
    reduce_g.core_done()
    w_z_copy = n.copy(w_out.at[w_own], w_out.at[w_own], n.at(z=z_far))
    reduce_z.first_done()
    reduce_g.first_done()
    reduce_c.first_done()
    y_z_copy.wait_recv()
    y_gather = [n.copy(y_out.at[y_half], y_out.at[y_half], n.at(y=n.step("y", k))) for k in (2, 1, 3)]
    reduce_z.second_done()
    reduce_g.second_done()
    w_z_copy.wait_recv()
    w_pair = n.rows(co_own, 512)
    w_gather = [n.copy(w_out.at[w_pair], w_out.at[w_pair], n.at(x=n.step("x", k))) for k in (2, 1, 3)]
    reduce_c.second_done()
    reduce_z.third_done()
    reduce_g.third_done()
    reduce_c.third_done()
    reduce_z.second_gathered()
    reduce_g.second_gathered()
    reduce_c.second_gathered()
    reduce_g.gathered()
    for c in w_gather:
        c.wait_recv()
    w_half = n.rows(n.c * 2048, 2048)
    w_core_copy = n.copy(w_out.at[w_half], w_out.at[w_half], n.partner)
    reduce_z.gathered()
    reduce_c.gathered()
    for c in y_gather:
        c.wait_recv()
    reduce_g.core_gathered()
    w_core_copy.wait_recv()
    reduce_c.core_gathered()
    reduce_z.core_gathered()
    for c in n.copies:
        c.wait_send()


def exchange(window, range_test, co_test, core_left, core_right):
    def f(*shape):
        return pltpu.VMEM(shape, F32)

    def b(*shape):
        return pltpu.VMEM(shape, BF16)

    def reduce_bufs(r):
        return [f(32 * r, 256), f(16 * r, 256), f(3, 4 * r, 256), f(3, r, 256), f(4, r, 256)]

    scratch = [
        f(4, 256, 2048), b(1024, 2048), b(1024, 2048), f(2048, 256), f(256, 1024), f(512, 1024), f(512, 2048),
        b(2048, 256), b(2048, 256), b(512, 1024), b(512, 1024), b(512, 1024), b(512, 2048), b(512, 2048),
        f(4096, 128), f(4, 512, 128), f(7, 256, 128),
        f(1024, 256), b(1024, 256), b(1024, 256), f(3, 256, 256), f(128, 256), b(1024, 512), b(1024, 512),
        *reduce_bufs(16), *reduce_bufs(32), *reduce_bufs(32),
        pltpu.SemaphoreType.DMA((8,)), pltpu.SemaphoreType.DMA((COPIES,)), pltpu.SemaphoreType.DMA((COPIES,)),
    ]
    return pl.pallas_call(
        exchange_kernel,
        out_shape=[jax.ShapeDtypeStruct(s, F32) for s in (
            (1024, 256), (4096, 128), (512, 256), (1024, 256), (1024, 256))],
        in_specs=[pl.BlockSpec(memory_space=pl.ANY)] * 5,
        out_specs=[pl.BlockSpec(memory_space=pltpu.VMEM)] * 5,
        scratch_shapes=scratch,
        compiler_params=pltpu.CompilerParams(collective_id=0, has_side_effects=True, vmem_limit_bytes=67043328),
        name="exchange",
    )(window, range_test, co_test, core_left, core_right)


QUAD = 8


def factor_panel(tiles):
    lane = lax.broadcasted_iota(jnp.int32, (8, 128), 1)
    sub = lax.broadcasted_iota(jnp.int32, (8, 128), 0)
    group = (lane // 32) * 32
    p = list(tiles)
    e = [jnp.where(sub + 8 * t == lane - group, 1.0, 0.0).astype(F32) for t in range(4)]
    pivots = [None] * 32

    def row(x, s):
        return jnp.broadcast_to(x[s:s + 1, :], (8, 128))

    for j in range(0, 32, QUAD):
        t0 = j // 8
        cols = [[jnp.take_along_axis(p[t], group + (j + k), axis=1) for t in range(t0, 4)] for k in range(QUAD)]
        rows = [row(p[t0], j % 8 + k) for k in range(QUAD)]
        rows_e = [row(e[t0], j % 8 + k) for k in range(QUAD)]
        s = [[row(cols[k][0], j % 8 + l) for l in range(QUAD)] for k in range(QUAD)]
        coefs = []
        for k in range(QUAD):
            d = s[k][k]
            pivots[j + k] = d
            inv = 1.0 / d
            for l in range(k + 1, QUAD):
                f = s[k][l] * inv
                for m in range(l, QUAD):
                    s[l][m] = s[l][m] - s[k][m] * f
                cols[l] = [a - b * f for a, b in zip(cols[l], cols[k])]
                rows[l] = rows[l] - rows[k] * f
                rows_e[l] = rows_e[l] - rows_e[k] * f
            coefs.append(inv)
        for i, t in enumerate(range(t0, 4)):
            for k in range(QUAD):
                coef = cols[k][i] * coefs[k]
                if t == t0:
                    coef = jnp.where(sub > j % 8 + k, coef, 0.0)
                p[t] = p[t] - coef * rows[k]
                e[t] = e[t] - coef * rows_e[k]
    out = []
    for t in range(4):
        d = pivots[8 * t]
        for s in range(1, 8):
            d = jnp.where(sub == s, pivots[8 * t + s], d)
        out.append(e[t] * (1.0 / jnp.sqrt(d)))
    return out


def stacked(left, right):
    both = mm(jnp.concatenate(left, axis=1), jnp.concatenate([right[0], right[0]], axis=0), NN)
    return both + mm(left[0], right[1], NN)


def final_kernel(
    y_hbm, w_hbm, gram, cyw, zed, rb_hbm, cb_hbm, core_ref, mat, y_ref, w_ref, rb_ref, cb_ref, mid, in_sem, out_sem
):
    loads = [pltpu.make_async_copy(y_hbm, y_ref, in_sem.at[0]), pltpu.make_async_copy(w_hbm, w_ref, in_sem.at[1])]
    for c in loads:
        c.start()
    lane = lax.broadcasted_iota(jnp.int32, (32, 128), 1)
    eye = (lax.broadcasted_iota(jnp.int32, (256, 256), 0) == lax.broadcasted_iota(jnp.int32, (256, 256), 1)).astype(F32)
    mat[0, :, 0:256] = gram[pl.ds(0, 256), :]
    mat[1, :, 0:256] = gram[pl.ds(256, 256), :]
    cy = split(cyw[pl.ds(0, 512), :])
    mat[2, :, 0:256] = mm3(cy, cy, TN)
    cw = [split(cyw[pl.ds(512 + 256 * k, 256), :]) for k in range(2)]
    mat[3, :, 0:256] = mm3(cw[0], cw[0], NT) + mm3(cw[1], cw[1], NT)
    for m in range(4):
        mat[m, :, 256:512] = eye
    for p in range(8):
        r0 = 32 * p
        c0 = r0 // 128 * 128
        e1 = 256 + (r0 + 32 + 127) // 128 * 128
        rows = slice(64 * p, 64 * p + 64)
        mid[rows, :] = (mm3(split(zed[64 * p:64 * p + 64, :]), cw[0], NT)
                        + mm3(split(zed[512 + 64 * p:512 + 64 * p + 64, :]), cw[1], NT))
        packed = None
        for m in range(4):
            block = mat[m, r0:r0 + 32, c0:c0 + 128]
            shift = (m * 32 - r0 % 128) % 128
            if shift:
                block = pltpu.roll(block, shift, axis=1)
            packed = block if packed is None else jnp.where(lane // 32 == m, block, packed)
        inverse = jnp.concatenate(factor_panel([packed[8 * t:8 * t + 8, :] for t in range(4)]), axis=0)
        left = jnp.concatenate([jnp.where(lane // 32 == m, inverse, 0.0) for m in range(4)], axis=0)
        right = jnp.concatenate([mat[m, r0:r0 + 32, c0:e1] for m in range(4)], axis=0)
        upper = stacked(split(left), split(right))
        for m in range(4):
            mat[m, r0:r0 + 32, c0:e1] = upper[32 * m:32 * m + 32, :]
        if p == 7:
            break
        b0 = (r0 + 32) // 128 * 128
        u_high, u_low = split(upper[:, b0 - c0:])
        below = split(upper[:, b0 - c0:256 - c0].T[r0 + 32 - b0:, :])
        zero = jnp.zeros((32, e1 - b0), BF16)
        for m in range(4):
            mine = [jnp.concatenate([u[32 * m:32 * m + 32] if k == m else zero for k in range(4)], axis=0)
                    for u in (u_high, u_low)]
            mat[m, r0 + 32:, b0:e1] = mat[m, r0 + 32:, b0:e1] - stacked(below, mine)
    keep = lax.broadcasted_iota(jnp.int32, (256, 256), 0) <= lax.broadcasted_iota(jnp.int32, (256, 256), 1)
    y_inv = split(mat[0, :, 256:512])
    w_inv = split(mat[1, :, 256:512])
    for c in loads:
        c.wait()
    stores = []
    for k in range(2):
        rows = slice(512 * k, 512 * k + 512)
        rb_ref[rows, :] = mm3(split(y_ref[rows, :]), y_inv, NT)
        stores.append(pltpu.make_async_copy(rb_ref.at[rows], rb_hbm.at[rows], out_sem.at[k]))
        stores[-1].start()
    for k in range(8):
        cols = slice(256 * k, 256 * k + 256)
        block = jnp.concatenate([w_ref[512 * k:512 * k + 256, :], w_ref[512 * k + 256:512 * k + 512, :]], axis=1)
        cb_ref[:, cols] = mm3(w_inv, split(block), NN)
        stores.append(pltpu.make_async_copy(cb_ref.at[:, cols], cb_hbm.at[:, cols], out_sem.at[2 + k]))
        stores[-1].start()
    up_y = jnp.where(keep, mat[0, :, 0:256], 0.0)
    up_w = jnp.where(keep, mat[1, :, 0:256], 0.0)
    l_inv = split(mat[2, :, 256:512])
    r_inv = split(mat[3, :, 256:512])
    inner = mm3(cy, split(mid[...]), TN)
    left = mm3f(up_y, mm3(l_inv, l_inv, TN), NN)
    right = mm3f(mm3(r_inv, r_inv, TN), up_w, NT)
    core_ref[...] = mm3f(mm3f(left, inner, NN), right, NN) * 16384.0
    for c in stores:
        c.wait()


def final(*parts):
    spec, hbm = pl.BlockSpec(memory_space=pltpu.VMEM), pl.BlockSpec(memory_space=pl.ANY)
    return pl.pallas_call(
        final_kernel,
        out_shape=[jax.ShapeDtypeStruct(s, F32) for s in ((1024, 256), (256, 2048), (256, 256))],
        in_specs=[hbm, hbm, spec, spec, spec],
        out_specs=[hbm, hbm, spec],
        scratch_shapes=[pltpu.VMEM(s, F32) for s in (
            (4, 256, 512), (1024, 256), (4096, 128), (1024, 256), (256, 2048), (512, 256))]
        + [pltpu.SemaphoreType.DMA((2,)), pltpu.SemaphoreType.DMA((10,))],
        compiler_params=pltpu.CompilerParams(vmem_limit_bytes=67043328),
        name="final",
    )(*parts)


def per_device(window, range_test, co_test, core_left, core_right):
    return tuple(final(*exchange(window, range_test, co_test, core_left, core_right)))


def solution(mesh):
    return jax.shard_map(
        per_device,
        mesh=mesh,
        in_specs=(P("cell", "tm"), P("tm", None), P(None, "cell"), P(None, "cell"), P(None, "tm")),
        out_specs=(P("cell", None), P(None, "tm"), P()),
        check_vma=False,
    )
```

```python
import functools
import math

import jax
import jax.numpy as jnp
from jax import lax
from jax.experimental import pallas as pl
from jax.experimental.pallas import tpu as pltpu
from jax.sharding import PartitionSpec as P

MESH = pl.DeviceIdType.MESH
F32 = jnp.float32
BF16 = jnp.bfloat16
NN = (((1,), (0,)), ((), ()))
NT = (((1,), (1,)), ((), ()))
TN = (((0,), (0,)), ((), ()))


def split(value):
    high = value.astype(BF16)
    low = (value - high.astype(F32)).astype(BF16)
    return high, low


def mm(left, right, dims):
    return lax.dot_general(left, right, dims, preferred_element_type=F32)


def mm3(left, right, dims):
    return mm(left[0], right[0], dims) + (mm(left[0], right[1], dims) + mm(left[1], right[0], dims))


def mm3f(left, right, dims):
    return mm3(split(left), split(right), dims)


def mmh(left, right, dims):
    return lax.dot_general(left, right, dims, precision=lax.Precision.HIGHEST, preferred_element_type=F32)


class Net:
    def __init__(self, send_sem, recv_sem):
        cell, tm = lax.axis_index("cell"), lax.axis_index("tm")
        self.x, self.zh, self.c = cell // 4, lax.rem(cell // 2, 2), lax.rem(cell, 2)
        self.y, self.zl = tm // 2, lax.rem(tm, 2)
        self.z = self.zh * 2 + self.zl
        self.flip = self.zh * 2 + 1 - self.zl
        self.partner = self.at(c=1 - self.c)
        self.send_sem, self.recv_sem = send_sem, recv_sem
        self.copies = []

    def at(self, x=None, y=None, z=None, c=None):
        x = self.x if x is None else x
        y = self.y if y is None else y
        c = self.c if c is None else c
        zh, zl = (self.zh, self.zl) if z is None else (z // 2, lax.rem(z, 2))
        return ((x * 2 + zh) * 2 + c, y * 2 + zl)

    def step(self, axis, k):
        return getattr(self, axis) if k == 0 else lax.rem(getattr(self, axis) + k, 4)

    def rows(self, start, size):
        return pl.ds(pl.multiple_of(start, 8), size)

    def copy(self, src, dst, device):
        k = len(self.copies)
        c = pltpu.make_async_remote_copy(
            src_ref=src, dst_ref=dst, send_sem=self.send_sem.at[k], recv_sem=self.recv_sem.at[k],
            device_id=device, device_id_type=MESH,
        )
        c.start()
        self.copies.append(c)
        return c


class Reduce:
    def __init__(self, net, axes, rows, source, out, core_in, first_in, second_in, third_in):
        self.net, self.axes, self.r = net, axes, rows
        self.source, self.out = source, out
        self.core_in, self.first_in, self.second_in, self.third_in = core_in, first_in, second_in, third_in

    def place(self, i=0, j=0):
        n, (a, b, _) = self.net, self.axes
        return n.c * 16 * self.r + (n.step(a, i) * 4 + n.step(b, j)) * self.r

    def block(self, i=0):
        n = self.net
        return n.rows(n.c * 16 * self.r + n.step(self.axes[0], i) * 4 * self.r, 4 * self.r)

    def peer(self, axis, k):
        return self.net.at(**{axis: self.net.step(axis, k)})

    def core_send(self):
        n, half = self.net, 16 * self.r
        self.c = n.copy(self.source.at[n.rows((1 - n.c) * half, half)], self.core_in, n.partner)

    def core_done(self):
        n, r = self.net, self.r
        self.c.wait_recv()
        own = n.rows(n.c * 16 * r, 16 * r)
        self.source[own, :] = self.source[own, :] + self.core_in[...]
        self.f = [n.copy(self.source.at[self.block(k)], self.first_in.at[i], self.peer(self.axes[0], k))
                  for i, k in enumerate((2, 1, 3))]

    def first_done(self):
        n, r = self.net, self.r
        for c in self.f:
            c.wait_recv()
        own = self.block()
        self.source[own, :] = (self.source[own, :] + self.first_in[0]) + (self.first_in[1] + self.first_in[2])
        self.s = [n.copy(self.source.at[n.rows(self.place(0, k), r)], self.second_in.at[i], self.peer(self.axes[1], k))
                  for i, k in enumerate((2, 1, 3))]

    def second_done(self):
        n, r = self.net, self.r
        for c in self.s:
            c.wait_recv()
        own = n.rows(self.place(), r)
        me = getattr(n, self.axes[2])
        self.third_in[me] = (self.source[own, :] + self.second_in[0]) + (self.second_in[1] + self.second_in[2])
        self.t = [n.copy(self.third_in.at[me], self.third_in.at[me], self.peer(self.axes[2], k)) for k in (2, 1, 3)]

    def third_done(self):
        n, r = self.net, self.r
        for c in self.t:
            c.wait_recv()
        own = n.rows(self.place(), r)
        self.out[own, :] = (self.third_in[0] + self.third_in[1]) + (self.third_in[2] + self.third_in[3])
        self.g = [n.copy(self.out.at[own], self.out.at[own], self.peer(self.axes[1], k)) for k in (2, 1, 3)]

    def second_gathered(self):
        n = self.net
        for c in self.g:
            c.wait_recv()
        own = self.block()
        self.h = [n.copy(self.out.at[own], self.out.at[own], self.peer(self.axes[0], k)) for k in (2, 1, 3)]

    def gathered(self):
        n, half = self.net, 16 * self.r
        for c in self.h:
            c.wait_recv()
        own = n.rows(n.c * half, half)
        self.c2 = n.copy(self.out.at[own], self.out.at[own], n.partner)

    def core_gathered(self):
        self.c2.wait_recv()


COPIES = 100
ORDER = (2, 1, 3, 0)
AXES = (("y", "x", "z"), ("x", "y", "z"), ("z", "y", "x"))


def meet(n):
    barrier = pltpu.get_barrier_semaphore()
    peers = [n.partner]
    for axis in "xyz":
        peers += [n.at(**{axis: n.step(axis, k)}) for k in (1, 2, 3)]
    peers += [n.at(x=n.step("x", k), z=n.step("z", 2)) for k in (1, 2, 3)]
    for peer in peers:
        pl.semaphore_signal(barrier, inc=1, device_id=peer, device_id_type=MESH)
    return barrier, len(peers)


def exchange_kernel(
    window, range_test, co_test, core_left, core_right,
    y_hbm, w_hbm, gram_hbm, cyw_hbm, z_hbm,
    y_out, w_out, gram_out, cyw_out, z_out,
    w_stage, w_hi, w_lo, rt_f, ct_f, cl_f, cr_f, rt_hi, rt_lo, ct2, cl_hi, cl_lo, cr_hi, cr_lo,
    co, co_core, co_in, rg, rg_hi, rg_lo, rg_in, rg_z, v_hi, v_lo,
    gram, g_core, g_first, g_second, g_third, cyw, c_core, c_first, c_second, c_third, zed, z_core, z_first, z_second, z_third,
    in_sem, out_sem, send_sem, recv_sem,
):
    n = Net(send_sem, recv_sem)
    barrier, greetings = meet(n)

    rows_of = [n.rows(n.step("y", k) * 256, 256) for k in ORDER]
    w_copies = [pltpu.make_async_copy(window.at[rows_of[s]], w_stage.at[s], in_sem.at[s]) for s in range(4)]
    loads = [pltpu.make_async_copy(a, b, in_sem.at[4 + i]) for i, (a, b) in enumerate(
        ((range_test, rt_f), (co_test, ct_f), (core_right, cr_f), (core_left, cl_f)))]
    loads[0].start()
    for c in w_copies[:2]:
        c.start()

    def split_rows(s):
        w_copies[s].wait()
        w_hi[rows_of[s], :], w_lo[rows_of[s], :] = split(w_stage[s])

    def range_block(s):
        rows = rows_of[s]
        value = mm3((w_hi[rows, :], w_lo[rows, :]), (rt_hi[...], rt_lo[...]), NN)
        rg[rows, :] = value
        rg_hi[rows, :], rg_lo[rows, :] = split(value)

    loads[0].wait()
    rt_hi[...], rt_lo[...] = split(rt_f[...])
    for c in w_copies[2:] + loads[1:2]:
        c.start()
    y_copies = []
    for s in range(3):
        split_rows(s)
        range_block(s)
        if s == 0:
            pl.semaphore_wait(barrier, greetings)
            loads[2].start()
        y_copies.append(n.copy(rg.at[rows_of[s]], rg_in.at[s], n.at(y=n.step("y", ORDER[s]))))
    loads[3].start()
    split_rows(3)

    loads[1].wait()
    ct2[0:256, :], ct2[256:512, :] = split(ct_f[...])

    def co_block(half, k):
        block = half * 4 + n.step("x", k)
        cols = pl.ds(pl.multiple_of(block * 256, 256), 256)
        both = mm(ct2[...], w_hi[:, cols], NN)
        value = (both[:256] + both[256:]) + mm(ct2[0:256, :], w_lo[:, cols], NN)
        co[n.rows(block * 512, 256), :] = value[:, :128]
        co[n.rows(block * 512 + 256, 256), :] = value[:, 128:]
        return n.rows(block * 512, 512)

    core_copies = []
    for s in range(4):
        at = co_block(1 - n.c, ORDER[s])
        core_copies.append(n.copy(co.at[at], co_core.at[s], n.partner))
    x_copies = []
    zh_far, z_far = 1 - n.zh, n.step("z", 2)
    for s in range(4):
        at = co_block(n.c, ORDER[s])
        core_copies[s].wait_recv()
        co[at, :] = co[at, :] + co_core[s]
        x = n.step("x", ORDER[s])
        base = (n.c * 4 + x) * 512
        x_copies.append(n.copy(co.at[n.rows(base + zh_far * 256, 256)], co_in.at[len(x_copies)], n.at(x=x, z=z_far)))
        if ORDER[s]:
            x_copies.append(n.copy(co.at[n.rows(base + n.zh * 256, 256)], co_in.at[len(x_copies)], n.at(x=x)))
    co_own = (n.c * 4 + n.x) * 512
    range_block(3)

    loads[2].wait()
    cr_hi[...], cr_lo[...] = split(cr_f[...])

    def v_block(k):
        rows = n.rows(k * 256, 256)
        value = mm3((w_hi[rows, :], w_lo[rows, :]), (cr_hi[...], cr_lo[...]), NT)
        v_hi[rows, :], v_lo[rows, :] = split(value)

    pl.loop(0, 3)(v_block)
    y_half = rows_of[3]
    total = rg[y_half, :]
    for k, c in enumerate(y_copies):
        c.wait_recv()
        total = total + rg_in[k]
    rg[y_half, :] = total
    z_flip = n.at(z=n.flip)
    rg_z_copy = n.copy(rg.at[n.rows(n.y * 256 + (1 - n.zl) * 128, 128)], rg_z, z_flip)
    pl.loop(3, 4)(v_block)

    loads[3].wait()
    cl_hi[...], cl_lo[...] = split(cl_f[...])
    left = (cl_hi[...], cl_lo[...])
    zed[pl.ds(0, 512), :] = mm3(left, (v_hi[:, 0:256], v_lo[:, 0:256]), NN)
    zed[pl.ds(512, 512), :] = mm3(left, (v_hi[:, 256:512], v_lo[:, 256:512]), NN)
    reduce_z = Reduce(n, AXES[2], 32, zed, z_out, z_core, z_first, z_second, z_third)
    reduce_z.core_send()
    cyw[pl.ds(0, 512), :] = mm3(left, (rg_hi[...], rg_lo[...]), NN)
    reduce_z.core_done()
    for k in range(2):
        cols = pl.ds(k * 256, 256)
        cyw[pl.ds(512 + 256 * k, 256), :] = mm3(
            (ct2[0:256, :], ct2[256:512, :]), (v_hi[:, cols], v_lo[:, cols]), NN)
    reduce_c = Reduce(n, AXES[1], 32, cyw, cyw_out, c_core, c_first, c_second, c_third)
    reduce_c.core_send()
    y_own = n.rows(n.y * 256 + n.zl * 128, 128)
    rg_z_copy.wait_recv()
    total = rg[y_own, :] + rg_z[...]
    y_out[y_own, :] = total
    part = split(total)
    gram[pl.ds(0, 256), :] = mm3(part, part, TN) * (1.0 / 16384)
    reduce_c.core_done()
    w_own = n.rows(co_own + n.zh * 256, 256)
    total = co[w_own, :]
    for k, c in enumerate(x_copies):
        c.wait_recv()
        total = total + co_in[k]
    w_out[w_own, :] = total
    part = split(total)
    gram[pl.ds(256, 256), :] = mm3(part, part, NT) * (1.0 / 16384)
    reduce_g = Reduce(n, AXES[0], 16, gram, gram_out, g_core, g_first, g_second, g_third)
    reduce_g.core_send()
    y_z_copy = n.copy(y_out.at[y_own], y_out.at[y_own], z_flip)
    reduce_g.core_done()
    w_z_copy = n.copy(w_out.at[w_own], w_out.at[w_own], n.at(z=z_far))
    reduce_z.first_done()
    reduce_g.first_done()
    reduce_c.first_done()
    y_z_copy.wait_recv()
    y_gather = [n.copy(y_out.at[y_half], y_out.at[y_half], n.at(y=n.step("y", k))) for k in (2, 1, 3)]
    reduce_z.second_done()
    reduce_g.second_done()
    w_z_copy.wait_recv()
    w_pair = n.rows(co_own, 512)
    w_gather = [n.copy(w_out.at[w_pair], w_out.at[w_pair], n.at(x=n.step("x", k))) for k in (2, 1, 3)]
    reduce_c.second_done()
    reduce_z.third_done()
    reduce_g.third_done()
    reduce_c.third_done()
    reduce_z.second_gathered()
    reduce_g.second_gathered()
    reduce_c.second_gathered()
    reduce_g.gathered()
    for c in w_gather:
        c.wait_recv()
    w_half = n.rows(n.c * 2048, 2048)
    w_core_copy = n.copy(w_out.at[w_half], w_out.at[w_half], n.partner)
    stores = []

    def store(src, dst):
        stores.append(pltpu.make_async_copy(src, dst, out_sem.at[len(stores)]))
        stores[-1].start()

    reduce_z.gathered()
    reduce_c.gathered()
    for c in y_gather:
        c.wait_recv()
    store(y_out, y_hbm)
    reduce_g.core_gathered()
    store(gram_out, gram_hbm)
    w_core_copy.wait_recv()
    store(w_out, w_hbm)
    reduce_z.core_gathered()
    store(z_out, z_hbm)
    reduce_c.core_gathered()
    store(cyw_out, cyw_hbm)
    for c in stores:
        c.wait()
    for c in n.copies:
        c.wait_send()


def exchange(window, range_test, co_test, core_left, core_right):
    def f(*shape):
        return pltpu.VMEM(shape, F32)

    def b(*shape):
        return pltpu.VMEM(shape, BF16)

    def reduce_bufs(r):
        return [f(32 * r, 256), f(16 * r, 256), f(3, 4 * r, 256), f(3, r, 256), f(4, r, 256)]

    scratch = [
        f(1024, 256), f(4096, 128), f(512, 256), f(1024, 256), f(1024, 256),
        f(4, 256, 2048), b(1024, 2048), b(1024, 2048), f(2048, 256), f(256, 1024), f(512, 1024), f(512, 2048),
        b(2048, 256), b(2048, 256), b(512, 1024), b(512, 1024), b(512, 1024), b(512, 2048), b(512, 2048),
        f(4096, 128), f(4, 512, 128), f(7, 256, 128),
        f(1024, 256), b(1024, 256), b(1024, 256), f(3, 256, 256), f(128, 256), b(1024, 512), b(1024, 512),
        *reduce_bufs(16), *reduce_bufs(32), *reduce_bufs(32),
        pltpu.SemaphoreType.DMA((8,)), pltpu.SemaphoreType.DMA((5,)), pltpu.SemaphoreType.DMA((COPIES,)), pltpu.SemaphoreType.DMA((COPIES,)),
    ]
    return pl.pallas_call(
        exchange_kernel,
        out_shape=[jax.ShapeDtypeStruct(s, F32) for s in (
            (1024, 256), (4096, 128), (512, 256), (1024, 256), (1024, 256))],
        in_specs=[pl.BlockSpec(memory_space=pl.ANY)] * 5,
        out_specs=[pl.BlockSpec(memory_space=pl.ANY)] * 5,
        scratch_shapes=scratch,
        compiler_params=pltpu.CompilerParams(collective_id=0, has_side_effects=True, vmem_limit_bytes=67043328),
        name="exchange",
    )(window, range_test, co_test, core_left, core_right)


QUAD = 8


def factor_panel(tiles):
    lane = lax.broadcasted_iota(jnp.int32, (8, 128), 1)
    sub = lax.broadcasted_iota(jnp.int32, (8, 128), 0)
    group = (lane // 32) * 32
    p = list(tiles)
    e = [jnp.where(sub + 8 * t == lane - group, 1.0, 0.0).astype(F32) for t in range(4)]
    pivots = [None] * 32

    def row(x, s):
        return jnp.broadcast_to(x[s:s + 1, :], (8, 128))

    for j in range(0, 32, QUAD):
        t0 = j // 8
        cols = [[jnp.take_along_axis(p[t], group + (j + k), axis=1) for t in range(t0, 4)] for k in range(QUAD)]
        rows = [row(p[t0], j % 8 + k) for k in range(QUAD)]
        rows_e = [row(e[t0], j % 8 + k) for k in range(QUAD)]
        s = [[row(cols[k][0], j % 8 + l) for l in range(QUAD)] for k in range(QUAD)]
        coefs = []
        for k in range(QUAD):
            d = s[k][k]
            pivots[j + k] = d
            inv = 1.0 / d
            for l in range(k + 1, QUAD):
                f = s[k][l] * inv
                for m in range(l, QUAD):
                    s[l][m] = s[l][m] - s[k][m] * f
                cols[l] = [a - b * f for a, b in zip(cols[l], cols[k])]
                rows[l] = rows[l] - rows[k] * f
                rows_e[l] = rows_e[l] - rows_e[k] * f
            coefs.append(inv)
        for i, t in enumerate(range(t0, 4)):
            for k in range(QUAD):
                coef = cols[k][i] * coefs[k]
                if t == t0:
                    coef = jnp.where(sub > j % 8 + k, coef, 0.0)
                p[t] = p[t] - coef * rows[k]
                e[t] = e[t] - coef * rows_e[k]
    out = []
    for t in range(4):
        d = pivots[8 * t]
        for s in range(1, 8):
            d = jnp.where(sub == s, pivots[8 * t + s], d)
        out.append(e[t] * (1.0 / jnp.sqrt(d)))
    return out


def stacked(left, right):
    both = mm(jnp.concatenate(left, axis=1), jnp.concatenate([right[0], right[0]], axis=0), NN)
    return both + mm(left[0], right[1], NN)


def final_kernel(
    y_hbm, w_hbm, gram, cyw, zed, rb_hbm, cb_hbm, core_ref, mat, y_ref, w_ref, rb_ref, cb_ref, mid, in_sem, out_sem
):
    loads = [pltpu.make_async_copy(y_hbm, y_ref, in_sem.at[0]), pltpu.make_async_copy(w_hbm, w_ref, in_sem.at[1])]
    for c in loads:
        c.start()
    lane = lax.broadcasted_iota(jnp.int32, (32, 128), 1)
    eye = (lax.broadcasted_iota(jnp.int32, (256, 256), 0) == lax.broadcasted_iota(jnp.int32, (256, 256), 1)).astype(F32)
    mat[0, :, 0:256] = gram[pl.ds(0, 256), :]
    mat[1, :, 0:256] = gram[pl.ds(256, 256), :]
    cy = split(cyw[pl.ds(0, 512), :])
    mat[2, :, 0:256] = mm3(cy, cy, TN)
    cw = [split(cyw[pl.ds(512 + 256 * k, 256), :]) for k in range(2)]
    mat[3, :, 0:256] = mm3(cw[0], cw[0], NT) + mm3(cw[1], cw[1], NT)
    for m in range(4):
        mat[m, :, 256:512] = eye
    for p in range(8):
        r0 = 32 * p
        c0 = r0 // 128 * 128
        e1 = 256 + (r0 + 32 + 127) // 128 * 128
        rows = slice(64 * p, 64 * p + 64)
        mid[rows, :] = (mm3(split(zed[64 * p:64 * p + 64, :]), cw[0], NT)
                        + mm3(split(zed[512 + 64 * p:512 + 64 * p + 64, :]), cw[1], NT))
        packed = None
        for m in range(4):
            block = mat[m, r0:r0 + 32, c0:c0 + 128]
            shift = (m * 32 - r0 % 128) % 128
            if shift:
                block = pltpu.roll(block, shift, axis=1)
            packed = block if packed is None else jnp.where(lane // 32 == m, block, packed)
        inverse = jnp.concatenate(factor_panel([packed[8 * t:8 * t + 8, :] for t in range(4)]), axis=0)
        left = jnp.concatenate([jnp.where(lane // 32 == m, inverse, 0.0) for m in range(4)], axis=0)
        right = jnp.concatenate([mat[m, r0:r0 + 32, c0:e1] for m in range(4)], axis=0)
        upper = stacked(split(left), split(right))
        for m in range(4):
            mat[m, r0:r0 + 32, c0:e1] = upper[32 * m:32 * m + 32, :]
        if p == 7:
            break
        b0 = (r0 + 32) // 128 * 128
        u_high, u_low = split(upper[:, b0 - c0:])
        below = split(upper[:, b0 - c0:256 - c0].T[r0 + 32 - b0:, :])
        zero = jnp.zeros((32, e1 - b0), BF16)
        for m in range(4):
            mine = [jnp.concatenate([u[32 * m:32 * m + 32] if k == m else zero for k in range(4)], axis=0)
                    for u in (u_high, u_low)]
            mat[m, r0 + 32:, b0:e1] = mat[m, r0 + 32:, b0:e1] - stacked(below, mine)
    keep = lax.broadcasted_iota(jnp.int32, (256, 256), 0) <= lax.broadcasted_iota(jnp.int32, (256, 256), 1)
    y_inv = split(mat[0, :, 256:512])
    w_inv = split(mat[1, :, 256:512])
    for c in loads:
        c.wait()
    stores = []
    for k in range(2):
        rows = slice(512 * k, 512 * k + 512)
        rb_ref[rows, :] = mm3(split(y_ref[rows, :]), y_inv, NT)
        stores.append(pltpu.make_async_copy(rb_ref.at[rows], rb_hbm.at[rows], out_sem.at[k]))
        stores[-1].start()
    for k in range(8):
        cols = slice(256 * k, 256 * k + 256)
        block = jnp.concatenate([w_ref[512 * k:512 * k + 256, :], w_ref[512 * k + 256:512 * k + 512, :]], axis=1)
        cb_ref[:, cols] = mm3(w_inv, split(block), NN)
        stores.append(pltpu.make_async_copy(cb_ref.at[:, cols], cb_hbm.at[:, cols], out_sem.at[2 + k]))
        stores[-1].start()
    up_y = jnp.where(keep, mat[0, :, 0:256], 0.0)
    up_w = jnp.where(keep, mat[1, :, 0:256], 0.0)
    l_inv = split(mat[2, :, 256:512])
    r_inv = split(mat[3, :, 256:512])
    inner = mm3(cy, split(mid[...]), TN)
    left = mm3f(up_y, mm3(l_inv, l_inv, TN), NN)
    right = mm3f(mm3(r_inv, r_inv, TN), up_w, NT)
    core_ref[...] = mm3f(mm3f(left, inner, NN), right, NN) * 16384.0
    for c in stores:
        c.wait()


def final(*parts):
    spec, hbm = pl.BlockSpec(memory_space=pltpu.VMEM), pl.BlockSpec(memory_space=pl.ANY)
    return pl.pallas_call(
        final_kernel,
        out_shape=[jax.ShapeDtypeStruct(s, F32) for s in ((1024, 256), (256, 2048), (256, 256))],
        in_specs=[hbm, hbm, spec, spec, spec],
        out_specs=[hbm, hbm, spec],
        scratch_shapes=[pltpu.VMEM(s, F32) for s in (
            (4, 256, 512), (1024, 256), (4096, 128), (1024, 256), (256, 2048), (512, 256))]
        + [pltpu.SemaphoreType.DMA((2,)), pltpu.SemaphoreType.DMA((10,))],
        compiler_params=pltpu.CompilerParams(vmem_limit_bytes=67043328),
        name="final",
    )(*parts)


def per_device(window, range_test, co_test, core_left, core_right):
    return tuple(final(*exchange(window, range_test, co_test, core_left, core_right)))


def solution(mesh):
    return jax.shard_map(
        per_device,
        mesh=mesh,
        in_specs=(P("cell", "tm"), P("tm", None), P(None, "cell"), P(None, "cell"), P(None, "tm")),
        out_specs=(P("cell", None), P(None, "tm"), P()),
        check_vma=False,
    )
```
